256 devices in a mesh: snap: 8 (over z), py: 4 (over y_lo, core), pz: 8 (over y_hi, x).
Axes of the slice: x: 4, y: 4 (y_hi: 2, y_lo: 2; y = y_hi * 2 + y_lo), z: 8, core: 2. Of those that a mesh axis runs over, the one named last changes fastest.
Arguments:
- velocity: bfloat16 [8, 3, 48, 384, 1024], P('snap', None, 'pz', 'py'), may hold values from -6 to 6
- metric_x: float32 [1024], replicated, may hold values from 0.5 to 2
- metric_y: float32 [384], replicated, may hold values from 0.3 to 3
- metric_z: float32 [48], replicated, may hold values from 0.5 to 2
- sketch_matrix: float32 [8, 4], replicated, may hold values from -2 to 2
Outputs:
- sketch: float32 [4, 3, 48, 384, 1024], P(None, None, None, ('snap', 'pz'), 'py')
The draws below stay inside these ranges and needn't reach their ends.
All inputs are finite; a program needn't handle non-finite values.
Results may differ from the reference program's by a relative error of at most 0.0065.
Values may be sent and summed in bfloat16 or wider, within the bound.
A program may use at most 128 MiB of HBM per device.

```python
import math
import jax
import jax.numpy as jnp
from jax import lax

NX = 1024
NY = 384
NZ = 48
RANK = 4
SNAPS = 8
ZBLOCK = 6
YBLOCK = 96


def draw_velocity(key, part):
    phase_key = jax.random.fold_in(key, 11)
    jitter_key = jax.random.fold_in(key, 12)
    value_key = jax.random.fold_in(key, 13)
    zblocks = NZ // ZBLOCK
    yblocks = NY // YBLOCK
    phase = jax.random.randint(phase_key, (), 0, 2)
    zindex = jnp.arange(NZ, dtype=jnp.int32) // ZBLOCK
    yindex = jnp.arange(NY, dtype=jnp.int32) // YBLOCK
    parity = (zindex[:, None] + yindex[None, :] + phase) % 2
    jitter = jax.random.uniform(jitter_key, (zblocks, yblocks), jnp.float32, -0.3, 0.0)
    jitter = jnp.repeat(jnp.repeat(jitter, ZBLOCK, axis=0), YBLOCK, axis=1)
    quiet_level = -3.9
    values = jax.random.truncated_normal(value_key, -6.0, 6.0, (SNAPS, 3, NZ, NY, NX), jnp.float32)
    log_level = jnp.where(parity == 1, 0.0, quiet_level) + jitter
    loudness = jnp.exp(log_level)[None, None, :, :, None]
    return (values * loudness).astype(jnp.bfloat16)


def centred(stream_key, shape, spread, bound, kind=jnp.bfloat16):
    return jnp.clip(spread * jax.random.normal(stream_key, shape, jnp.float32), -bound, bound).astype(kind)


def setup_inputs(seed: int = 0) -> dict:
    splits = jax.random.split(jax.random.key(seed), 6)
    velocity = draw_velocity(jax.random.fold_in(splits[5], 71), 0)
    metric_x = jnp.clip(jnp.exp(jax.random.uniform(splits[1], (NX,), jnp.float32, math.log(0.5), math.log(2.0))), 0.5, 2.0)
    metric_y = jnp.clip(jnp.exp(jax.random.uniform(splits[2], (NY,), jnp.float32, math.log(0.3), math.log(3.0))), 0.3, 3.0)
    metric_z = jnp.clip(jnp.exp(jax.random.uniform(splits[3], (NZ,), jnp.float32, math.log(0.5), math.log(2.0))), 0.5, 2.0)
    sketch_matrix = centred(splits[4], (SNAPS, RANK), SNAPS ** -0.5, 2.0, jnp.float32)
    return dict(velocity=velocity, metric_x=metric_x, metric_y=metric_y, metric_z=metric_z, sketch_matrix=sketch_matrix)


def line_derivative(field, axis):
    moved = jnp.moveaxis(field, axis, 0)
    points = moved.shape[0]
    flattened = moved.reshape(points, -1)
    padded = jnp.pad(flattened, ((2, 2), (0, 0)))
    right_side = 7.0 / 9.0 * (padded[3:points + 3] - padded[1:points + 1]) + 1.0 / 36.0 * (padded[4:points + 4] - padded[0:points])
    lower_band = jnp.full((points,), 1.0 / 3.0, right_side.dtype).at[0].set(0.0)
    upper_band = jnp.full((points,), 1.0 / 3.0, right_side.dtype).at[points - 1].set(0.0)
    main_band = jnp.ones((points,), right_side.dtype)
    solved = lax.linalg.tridiagonal_solve(lower_band, main_band, upper_band, right_side)
    return jnp.moveaxis(solved.reshape(moved.shape), 0, axis)

def reference(velocity, metric_x, metric_y, metric_z, sketch_matrix):
    scale_x = metric_x[None, None, :]
    scale_y = metric_y[None, :, None]
    scale_z = metric_z[:, None, None]

    def one_snapshot(total, inputs):
        snapshot, weights = inputs
        vel_u = snapshot[0].astype(jnp.float32)
        vel_v = snapshot[1].astype(jnp.float32)
        vel_w = snapshot[2].astype(jnp.float32)
        slope_vx = (scale_x * line_derivative(vel_v, 2)).astype(jnp.bfloat16)
        slope_wx = (scale_x * line_derivative(vel_w, 2)).astype(jnp.bfloat16)
        slope_uy = scale_y * line_derivative(vel_u, 1)
        slope_wy = (scale_y * line_derivative(vel_w, 1)).astype(jnp.bfloat16)
        spin_z = (slope_vx.astype(jnp.float32) - slope_uy).astype(jnp.bfloat16)
        slope_uz = scale_z * line_derivative(vel_u, 0)
        slope_vz = scale_z * line_derivative(vel_v, 0)
        spin_x = (slope_wy.astype(jnp.float32) - slope_vz).astype(jnp.bfloat16)
        spin_y = (slope_uz - slope_wx.astype(jnp.float32)).astype(jnp.bfloat16)
        vorticity = jnp.stack([spin_x, spin_y, spin_z], axis=0).astype(jnp.float32)
        term = weights.astype(jnp.float32)[:, None, None, None, None] * vorticity[None]
        return (total + term, None)
    start = jnp.zeros((RANK, 3, NZ, NY, NX), jnp.float32)
    total, unused = lax.scan(one_snapshot, start, (velocity, sketch_matrix))
    return total
```

```python
import functools

import jax
import jax.numpy as jnp
import numpy as np
from jax import lax
from jax.experimental import pallas as pl
from jax.experimental.pallas import tpu as pltpu
from jax.sharding import PartitionSpec as P

MESH = pl.DeviceIdType.MESH
F32 = jnp.float32
BF16 = jnp.bfloat16
LANES = 128
NUMS = 8


def tridiagonal(n):
    return np.eye(n) + (np.eye(n, k=1) + np.eye(n, k=-1)) / 3.0


def right_side(n):
    first = np.eye(n, k=1) - np.eye(n, k=-1)
    second = np.eye(n, k=2) - np.eye(n, k=-2)
    return 7.0 / 9.0 * first + 1.0 / 36.0 * second


def derivative(n):
    return np.linalg.solve(tridiagonal(n), right_side(n))


def block_table(n):
    halo = np.zeros((n, NUMS))
    halo[0, 0], halo[0, 1], halo[1, 1] = -1.0 / 36.0, -7.0 / 9.0, -1.0 / 36.0
    halo[n - 1, 2], halo[n - 2, 2], halo[n - 1, 3] = 7.0 / 9.0, 1.0 / 36.0, 1.0 / 36.0
    halo[0, 4:6] = -1.0 / 3.0
    halo[n - 1, 6:8] = -1.0 / 3.0
    return np.linalg.solve(tridiagonal(n), np.concatenate([right_side(n), halo], axis=1))


def interface_rows(n, blocks):
    whole, size = derivative(n), n // blocks
    rows = np.zeros((blocks, NUMS, n))
    for block in range(blocks):
        low, high = block * size, (block + 1) * size
        if block > 0:
            rows[block, 0, low - 2] = 1.0
            rows[block, 1, low - 1] = 1.0
            rows[block, 4] = rows[block, 5] = whole[low - 1]
        if block < blocks - 1:
            rows[block, 2, high] = 1.0
            rows[block, 3, high + 1] = 1.0
            rows[block, 6] = rows[block, 7] = whole[high]
    return rows.reshape(blocks * NUMS, n)


def split(table):
    high = np.asarray(table, np.float32).astype(BF16)
    low = (np.asarray(table, np.float64) - high.astype(np.float64)).astype(BF16)
    return np.stack([high, low])


def dot(left, right):
    return jnp.dot(left, right, preferred_element_type=F32)


def halves(value):
    high = value.astype(BF16)
    return high, (value - high.astype(F32)).astype(BF16)


def sizes_of(mesh, shape, rank):
    snaps, nyblocks, nzblocks = mesh.shape["snap"], mesh.shape["py"], mesh.shape["pz"]
    nz, ny, nx = shape[2:]
    return dict(
        S=snaps, PY=nyblocks, PZ=nzblocks, K=rank, ZB=nz // nzblocks, YB=ny // nyblocks,
        XB=nx // nyblocks, RY=ny // snaps, RG=ny // snaps // nzblocks, NX=nx, NY=ny, NZ=nz,
    )


def tables_of(z):
    S, PY, PZ, K, RY, RG, XB, NZ = (z[n] for n in ("S", "PY", "PZ", "K", "RY", "RG", "XB", "NZ"))
    gx = np.zeros((z["NX"], LANES))
    gx[:, : PY * NUMS] = interface_rows(z["NX"], PY).T
    gy = interface_rows(z["NY"], S)
    bx, by = block_table(XB), block_table(RY)
    tx = np.zeros((2, XB + LANES, XB))
    ty = np.zeros((2, RY, RY + 16))
    for f in range(2):
        tx[f, :XB] = bx[:, :XB].T
        tx[f, XB + NUMS * f : XB + NUMS * (f + 1)] = bx[:, XB:].T
        ty[f, :, :RY] = by[:, :RY]
        ty[f, :, RY + NUMS * f : RY + NUMS * (f + 1)] = by[:, RY:]
    dz = np.einsum("zw,ij->izwj", derivative(NZ), np.eye(8)).reshape(8 * NZ, 8 * NZ)
    turn = np.einsum("zw,ij->izwj", np.eye(NZ), np.eye(8)).reshape(8 * NZ, 8 * NZ)
    rows = 2 * K * RY
    gather = np.zeros((rows, rows))
    groups = K * RG // 8
    for zz in range(2):
        for k in range(K):
            for q in range(PZ):
                for r in range(RG):
                    g, i = divmod(k * RG + r, 8)
                    gather[((q * groups + g) * 2 + zz) * 8 + i, (zz * K + k) * RY + q * RG + r] = 1.0
    one = lambda t: jnp.asarray(t.astype(np.float32)).astype(BF16)
    return [jnp.asarray(split(t)) for t in (gx, gy, tx, ty, dz)] + [one(turn), one(gather)]


def body(
    z, vel, gx, gy, tx, ty, dz, turn, gather, mx, my, mz, sk, out,
    vw, ef, es, buf_a, buf_e, buf_y, buf_c, buf_cy, buf_ce, se, xh, xl, yh, yl, pb, buf_bs, buf_r,
    send_a, recv_a, send_e, recv_e, send_c, recv_c, send_cy, recv_cy, send_ce, recv_ce, send_b, recv_b,
    local_v, local_a, local_e, local_c, local_cy, local_ce, local_b,
):
    S, PY, PZ, K, ZB, YB, XB, RY, RG = (z[n] for n in ("S", "PY", "PZ", "K", "ZB", "YB", "XB", "RY", "RG"))
    groups, fields = K * RG // 8, 7
    me_s, me_y, me_z = lax.axis_index("snap"), lax.axis_index("py"), lax.axis_index("pz")

    def other(me, d, n):
        return lax.rem(me + d, n)

    def remote(src, dst, send, recv, axis, peer):
        return pltpu.make_async_remote_copy(
            src_ref=src, dst_ref=dst, send_sem=send, recv_sem=recv, device_id={axis: peer}, device_id_type=MESH)

    def mult(value, size):
        return pl.ds(pl.multiple_of(value * size, size), size)

    def a_copy(p, d):
        peer = other(me_y, d, PY)
        return remote(vel.at[0, :, p, :, mult(peer, XB)], buf_a.at[p, :, mult(me_y, YB), :],
                      send_a.at[p, d - 1], recv_a.at[p, d - 1], "py", peer)

    def a_local(p):
        return pltpu.make_async_copy(vel.at[0, :, p, :, mult(me_y, XB)], buf_a.at[p, :, mult(me_y, YB), :], local_a.at[p])

    def e_copy(d):
        peer = other(me_y, d, PY)
        return remote(es.at[peer], buf_e.at[mult(me_y, YB), :], send_e.at[d - 1], recv_e.at[d - 1], "py", peer)

    def e_local():
        return pltpu.make_async_copy(es.at[me_y], buf_e.at[mult(me_y, YB), :], local_e.at[0])

    def c_copy(p, d):
        peer = other(me_s, d, S)
        return remote(buf_a.at[p, :, mult(peer, RY), :], buf_c.at[me_s, p],
                      send_c.at[p, d - 1], recv_c.at[p, d - 1], "snap", peer)

    def c_local(p):
        return pltpu.make_async_copy(buf_a.at[p, :, mult(me_s, RY), :], buf_c.at[me_s, p], local_c.at[p])

    def cy_copy(p, d):
        peer = other(me_s, d, S)
        return remote(buf_y.at[p, peer], buf_cy.at[me_s, p],
                      send_cy.at[p, d - 1], recv_cy.at[p, d - 1], "snap", peer)

    def cy_local(p):
        return pltpu.make_async_copy(buf_y.at[p, me_s], buf_cy.at[me_s, p], local_cy.at[p])

    def ce_copy(d):
        peer = other(me_s, d, S)
        return remote(buf_e.at[mult(peer, RY), :], buf_ce.at[me_s], send_ce.at[d - 1], recv_ce.at[d - 1], "snap", peer)

    def ce_local():
        return pltpu.make_async_copy(buf_e.at[mult(me_s, RY), :], buf_ce.at[me_s], local_ce.at[0])

    def b_rows(pp):
        return pl.ds(pl.multiple_of((me_z * (ZB // 2) + pp) * 16, 16), 16)

    def b_copy(pp, d):
        peer = other(me_z, d, PZ)
        return remote(buf_bs.at[pp, peer], buf_r.at[:, b_rows(pp), :],
                      send_b.at[pp, d - 1], recv_b.at[pp, d - 1], "pz", peer)

    def b_local(pp):
        return pltpu.make_async_copy(buf_bs.at[pp, me_z], buf_r.at[:, b_rows(pp), :], local_b.at[pp])

    planes_in = pltpu.make_async_copy(vel.at[0, 1:3], vw, local_v.at[0])
    planes_in.start()
    for p in range(ZB):
        a_local(p).start()

    barrier = pltpu.get_barrier_semaphore()
    for axis, me, n in (("py", me_y, PY), ("snap", me_s, S), ("pz", me_z, PZ)):
        for d in range(1, n):
            pl.semaphore_signal(barrier, inc=1, device_id={axis: other(me, d, n)}, device_id_type=MESH)
    pl.semaphore_wait(barrier, PY + S + PZ - 3)

    for p in range(ZB):
        for d in range(1, PY):
            a_copy(p, d).start()

    planes_in.wait()
    lane = lax.broadcasted_iota(jnp.int32, (YB, LANES), 1)
    for f in range(2):
        for p in range(ZB):
            j = 2 * p + f
            line = vw[f, p]
            ef[j] = dot(line, gx[0]) + dot(line, gx[1])
    for b in range(PY):
        total = jnp.zeros((YB, LANES), F32)
        for j in range(2 * ZB):
            shifted = pltpu.roll(ef[j], (NUMS * (j - b)) % LANES, 1)
            total = jnp.where((lane >= NUMS * j) & (lane < NUMS * (j + 1)), shifted, total)
        rounded = total.astype(BF16).astype(F32)
        low = (lane % NUMS == 5) | (lane % NUMS == 7)
        es[b] = jnp.where(low, total - rounded, rounded).astype(BF16)
    for d in range(1, PY):
        e_copy(d).start()
    e_local().start()

    def a_stage(p):
        a_local(p).wait()
        for d in range(1, PY):
            a_copy(p, d).wait_recv()
        row = lax.broadcasted_iota(jnp.int32, (S * NUMS, XB), 0)
        low = (row % NUMS == 5) | (row % NUMS == 7)
        parts = []
        for f in (0, 2):
            field = buf_a[p, f]
            numbers = dot(gy[0], field) + dot(gy[1], field)
            rounded = numbers.astype(BF16).astype(F32)
            parts.append(jnp.where(low, numbers - rounded, rounded))
        for s in range(S):
            cut = slice(NUMS * s, NUMS * (s + 1))
            buf_y[p, s] = jnp.concatenate([parts[0][cut], parts[1][cut]], axis=0).astype(BF16)
        for d in range(1, S):
            c_copy(p, d).start()
            cy_copy(p, d).start()
        c_local(p).start()
        cy_local(p).start()

    def e_stage():
        e_local().wait()
        for d in range(1, PY):
            e_copy(d).wait_recv()
        for d in range(1, S):
            ce_copy(d).start()
        ce_local().start()

    def se_stage():
        ce_local().wait()
        for d in range(1, S):
            ce_copy(d).wait_recv()
        for k in range(K):
            total = sk[0, k] * buf_ce[0].astype(F32)
            for s in range(1, S):
                total = total + sk[s, k] * buf_ce[s].astype(F32)
            se[RY * k : RY * (k + 1), :] = total

    def s_stage(p):
        c_local(p).wait()
        cy_local(p).wait()
        for d in range(1, S):
            c_copy(p, d).wait_recv()
            cy_copy(p, d).wait_recv()
        base = lax.rem(p, 2) * (K * RY)

        def sketch(parts, k):
            total = sk[0, k] * parts[0]
            for s in range(1, S):
                total = total + sk[s, k] * parts[s]
            return halves(total)

        for f in range(3):
            for t in range(RY // 16):
                rows = slice(16 * t, 16 * (t + 1))
                parts = [buf_c[s, p, f, rows, :].astype(F32) for s in range(S)]
                for k in range(K):
                    high, low = sketch(parts, k)
                    if f != 1:
                        yh[f // 2, rows, XB * k : XB * (k + 1)] = high
                        yl[f // 2, rows, XB * k : XB * (k + 1)] = low
                    own = slice(RY * k + 16 * t, RY * k + 16 * (t + 1))
                    if f != 0:
                        xh[f - 1, own, :XB] = high
                        xl[f - 1, own, :XB] = low
                    if f != 2:
                        dest = pl.ds(pl.multiple_of(base + RY * k + 16 * t, 16), 16)
                        pb[2 * f, dest, :] = high
                        pb[2 * f + 1, dest, :] = low
        parts = [buf_cy[s, p].astype(F32) for s in range(S)]
        for k in range(K):
            high, low = sketch(parts, k)
            for f in range(2):
                yh[f, RY : RY + 16, XB * k : XB * (k + 1)] = high
                yl[f, RY : RY + 16, XB * k : XB * (k + 1)] = low
        high, low = halves(pltpu.roll(se[...], lax.rem(LANES - 2 * NUMS * p, LANES), 1))
        for f in range(2):
            xh[f, :, XB:] = high
            xl[f, :, XB:] = low

        x_slopes = [dot(xh[f], tx[0, f]) + dot(xl[f], tx[0, f]) + dot(xh[f], tx[1, f]) for f in range(2)]
        y_slopes = [dot(ty[0, f], yh[f]) + dot(ty[0, f], yl[f]) + dot(ty[1, f], yh[f]) for f in range(2)]
        scale_x = mx[0:1, mult(me_y, XB)]
        scale_y = jnp.tile(my[mult(me_s, RY), :], (1, XB // LANES))
        for k in range(K):
            own, cols = slice(RY * k, RY * (k + 1)), slice(XB * k, XB * (k + 1))
            dest = pl.ds(pl.multiple_of(base + RY * k, 16), RY)
            pb[4, dest, :] = (x_slopes[1][own] * scale_x).astype(BF16)
            pb[5, dest, :] = (y_slopes[1][:, cols] * scale_y).astype(BF16)
            pb[6, dest, :] = (x_slopes[0][own] * scale_x - y_slopes[0][:, cols] * scale_y).astype(BF16)

        @pl.when(lax.rem(p, 2) == 1)
        def _():
            pp = p // 2
            for f in range(fields):
                moved = dot(gather[...], pb[f]).astype(BF16)
                for q in range(PZ):
                    for g in range(groups):
                        cut = (q * groups + g) * 16
                        buf_bs[pp, q, g * fields + f] = moved[cut : cut + 16]
            for d in range(1, PZ):
                b_copy(pp, d).start()
            b_local(pp).start()

    lag = min(3, ZB)

    @pl.loop(0, ZB + lag)
    def _(i):
        @pl.when(i < ZB)
        def _():
            a_stage(i)

        @pl.when(i == 1)
        def _():
            e_stage()

        @pl.when(i == lag)
        def _():
            se_stage()

        @pl.when(i >= lag)
        def _():
            s_stage(i - lag)

    for pp in range(ZB // 2):
        b_local(pp).wait()
        for d in range(1, PZ):
            b_copy(pp, d).wait_recv()
    NZ = z["NZ"]
    scale_z = jnp.tile(mz[...], (1, XB // LANES))
    for g in range(groups):
        at = g * fields
        slope = [
            dot(dz[0], buf_r[at + 2 * f]) + dot(dz[0], buf_r[at + 2 * f + 1]) + dot(dz[1], buf_r[at + 2 * f]) for f in range(2)
        ]
        w_x, w_y, spin_z = (dot(turn[...], buf_r[at + f]) for f in (4, 5, 6))
        for i in range(8):
            k, r = divmod(8 * g + i, RG)
            cut = slice(NZ * i, NZ * (i + 1))
            out[k, 0, r] = w_y[cut] - slope[1][cut] * scale_z
            out[k, 1, r] = slope[0][cut] * scale_z - w_x[cut]
            out[k, 2, r] = spin_z[cut]

    for p in range(ZB):
        for d in range(1, PY):
            a_copy(p, d).wait_send()
        for d in range(1, S):
            c_copy(p, d).wait_send()
            cy_copy(p, d).wait_send()
    for d in range(1, PY):
        e_copy(d).wait_send()
    for d in range(1, S):
        ce_copy(d).wait_send()
    for pp in range(ZB // 2):
        for d in range(1, PZ):
            b_copy(pp, d).wait_send()


def solution(mesh):
    def step(velocity, metric_x, metric_y, metric_z, sketch_matrix):
        whole = (1, 3, velocity.shape[2] * mesh.shape["pz"], velocity.shape[3] * mesh.shape["py"], velocity.shape[4])
        z = sizes_of(mesh, whole, sketch_matrix.shape[1])
        S, PY, PZ, K, ZB, YB, XB, RY, RG, NX, NY, NZ = (z[n] for n in (
            "S", "PY", "PZ", "K", "ZB", "YB", "XB", "RY", "RG", "NX", "NY", "NZ"))
        tables = tables_of(z)
        my = jnp.broadcast_to(metric_y[:, None], (NY, LANES))
        mz = jnp.broadcast_to(metric_z[:, None], (NZ, LANES))
        groups, fields = K * RG // 8, 7
        dma = pltpu.SemaphoreType.DMA
        vmem = pl.BlockSpec(memory_space=pltpu.VMEM)
        result = pl.pallas_call(
            functools.partial(body, z),
            out_shape=jax.ShapeDtypeStruct((K, 3, RG, NZ, XB), F32),
            in_specs=[pl.BlockSpec(memory_space=pl.ANY)] + [vmem] * 10 + [pl.BlockSpec(memory_space=pltpu.SMEM)],
            out_specs=vmem,
            scratch_shapes=[
                pltpu.VMEM((2, ZB, YB, NX), BF16),
                pltpu.VMEM((2 * ZB, YB, LANES), F32),
                pltpu.VMEM((PY, YB, LANES), BF16),
                pltpu.VMEM((ZB, 3, NY, XB), BF16),
                pltpu.VMEM((NY, LANES), BF16),
                pltpu.VMEM((ZB, S, 16, XB), BF16),
                pltpu.VMEM((S, ZB, 3, RY, XB), BF16),
                pltpu.VMEM((S, ZB, 16, XB), BF16),
                pltpu.VMEM((S, RY, LANES), BF16),
                pltpu.VMEM((K * RY, LANES), F32),
                pltpu.VMEM((2, K * RY, XB + LANES), BF16),
                pltpu.VMEM((2, K * RY, XB + LANES), BF16),
                pltpu.VMEM((2, RY + 16, K * XB), BF16),
                pltpu.VMEM((2, RY + 16, K * XB), BF16),
                pltpu.VMEM((fields, 2 * K * RY, XB), BF16),
                pltpu.VMEM((ZB // 2, PZ, groups * fields, 16, XB), BF16),
                pltpu.VMEM((groups * fields, 8 * NZ, XB), BF16),
                dma((ZB, PY - 1)), dma((ZB, PY - 1)), dma((PY - 1,)), dma((PY - 1,)),
                dma((ZB, S - 1)), dma((ZB, S - 1)), dma((ZB, S - 1)), dma((ZB, S - 1)),
                dma((S - 1,)), dma((S - 1,)), dma((ZB // 2, PZ - 1)), dma((ZB // 2, PZ - 1)),
                dma((1,)), dma((ZB,)), dma((1,)), dma((ZB,)), dma((ZB,)), dma((1,)), dma((ZB // 2,)),
            ],
            compiler_params=pltpu.CompilerParams(
                collective_id=0, has_side_effects=True, vmem_limit_bytes=60 * 1024 * 1024),
        )(velocity, *tables, metric_x[None, :], my, mz, sketch_matrix)
        return jnp.swapaxes(result, 2, 3)

    return jax.shard_map(
        step,
        mesh=mesh,
        in_specs=(P("snap", None, "pz", "py", None), P(), P(), P(), P()),
        out_specs=P(None, None, None, ("snap", "pz"), "py"),
        check_vma=False,
    )
```

```python
import functools

import jax
import jax.numpy as jnp
import numpy as np
from jax import lax
from jax.experimental import pallas as pl
from jax.experimental.pallas import tpu as pltpu
from jax.sharding import PartitionSpec as P

MESH = pl.DeviceIdType.MESH
F32 = jnp.float32
BF16 = jnp.bfloat16
LANES = 128
NUMS = 8


def tridiagonal(n):
    return np.eye(n) + (np.eye(n, k=1) + np.eye(n, k=-1)) / 3.0


def right_side(n):
    first = np.eye(n, k=1) - np.eye(n, k=-1)
    second = np.eye(n, k=2) - np.eye(n, k=-2)
    return 7.0 / 9.0 * first + 1.0 / 36.0 * second


def derivative(n):
    return np.linalg.solve(tridiagonal(n), right_side(n))


def block_table(n):
    halo = np.zeros((n, NUMS))
    halo[0, 0], halo[0, 1], halo[1, 1] = -1.0 / 36.0, -7.0 / 9.0, -1.0 / 36.0
    halo[n - 1, 2], halo[n - 2, 2], halo[n - 1, 3] = 7.0 / 9.0, 1.0 / 36.0, 1.0 / 36.0
    halo[0, 4:6] = -1.0 / 3.0
    halo[n - 1, 6:8] = -1.0 / 3.0
    return np.linalg.solve(tridiagonal(n), np.concatenate([right_side(n), halo], axis=1))


def interface_rows(n, blocks):
    whole, size = derivative(n), n // blocks
    rows = np.zeros((blocks, NUMS, n))
    for block in range(blocks):
        low, high = block * size, (block + 1) * size
        if block > 0:
            rows[block, 0, low - 2] = 1.0
            rows[block, 1, low - 1] = 1.0
            rows[block, 4] = rows[block, 5] = whole[low - 1]
        if block < blocks - 1:
            rows[block, 2, high] = 1.0
            rows[block, 3, high + 1] = 1.0
            rows[block, 6] = rows[block, 7] = whole[high]
    return rows.reshape(blocks * NUMS, n)


def split(table):
    high = np.asarray(table, np.float32).astype(BF16)
    low = (np.asarray(table, np.float64) - high.astype(np.float64)).astype(BF16)
    return np.stack([high, low])


def dot(left, right):
    return jnp.dot(left, right, preferred_element_type=F32)


def halves(value):
    high = value.astype(BF16)
    return high, (value - high.astype(F32)).astype(BF16)


def sizes_of(mesh, shape, rank):
    snaps, nyblocks, nzblocks = mesh.shape["snap"], mesh.shape["py"], mesh.shape["pz"]
    nz, ny, nx = shape[2:]
    return dict(
        S=snaps, PY=nyblocks, PZ=nzblocks, K=rank, ZB=nz // nzblocks, YB=ny // nyblocks,
        XB=nx // nyblocks, RY=ny // snaps, RG=ny // snaps // nzblocks, NX=nx, NY=ny, NZ=nz,
    )


def tables_of(z):
    S, PY, PZ, K, RY, RG, XB, NZ = (z[n] for n in ("S", "PY", "PZ", "K", "RY", "RG", "XB", "NZ"))
    gx = np.zeros((z["NX"], LANES))
    gx[:, : PY * NUMS] = interface_rows(z["NX"], PY).T
    gy = interface_rows(z["NY"], S)
    bx, by = block_table(XB), block_table(RY)
    tx = np.zeros((2, XB + LANES, XB))
    ty = np.zeros((2, RY, RY + 16))
    for f in range(2):
        tx[f, :XB] = bx[:, :XB].T
        tx[f, XB + NUMS * f : XB + NUMS * (f + 1)] = bx[:, XB:].T
        ty[f, :, :RY] = by[:, :RY]
        ty[f, :, RY + NUMS * f : RY + NUMS * (f + 1)] = by[:, RY:]
    dz = np.einsum("zw,ij->izwj", derivative(NZ), np.eye(8)).reshape(8 * NZ, 8 * NZ)
    turn = np.einsum("zw,ij->izwj", np.eye(NZ), np.eye(8)).reshape(8 * NZ, 8 * NZ)
    gather = np.zeros((K * RY, K * RY))
    groups = K * RG // 8
    for k in range(K):
        for q in range(PZ):
            for r in range(RG):
                g, i = divmod(r * K + k, 8)
                gather[(q * groups + g) * 8 + i, k * RY + q * RG + r] = 1.0
    one = lambda t: jnp.asarray(t.astype(np.float32)).astype(BF16)
    return [jnp.asarray(split(t)) for t in (gx, gy, tx, ty)] + [one(gather)], [jnp.asarray(split(dz)), one(turn)]


def body(
    z, vel, gx_in, gy_in, tx_in, ty_in, gather_in, mx, my, sk, out,
    gx, gy, tx, ty, gather, scale_y,
    vw, ef, es, buf_a, buf_e, buf_y, buf_c, buf_cy, buf_ce, se, xh, xl, yh, yl, pb, buf_bs,
    send_a, recv_a, send_e, recv_e, send_c, recv_c, send_cy, recv_cy, send_ce, recv_ce, send_b, recv_b,
    local_t, local_v, local_a, local_e, local_c, local_cy, local_ce, local_b,
):
    S, PY, PZ, K, ZB, YB, XB, RY, RG = (z[n] for n in ("S", "PY", "PZ", "K", "ZB", "YB", "XB", "RY", "RG"))
    groups, fields = K * RG // 8, 7
    me_s, me_y, me_z = lax.axis_index("snap"), lax.axis_index("py"), lax.axis_index("pz")

    def other(me, d, n):
        return lax.rem(me + d, n)

    def remote(src, dst, send, recv, axis, peer):
        return pltpu.make_async_remote_copy(
            src_ref=src, dst_ref=dst, send_sem=send, recv_sem=recv, device_id={axis: peer}, device_id_type=MESH)

    def mult(value, size):
        return pl.ds(pl.multiple_of(value * size, size), size)

    def a_copy(p, f, d):
        peer = other(me_y, d, PY)
        return remote(vel.at[0, f, p, :, mult(peer, XB)], buf_a.at[p, f, mult(me_y, YB), :],
                      send_a.at[p, f, d - 1], recv_a.at[p, f, d - 1], "py", peer)

    def a_local(p):
        return pltpu.make_async_copy(vel.at[0, :, p, :, mult(me_y, XB)], buf_a.at[p, :, mult(me_y, YB), :], local_a.at[p])

    def e_copy(d):
        peer = other(me_y, d, PY)
        return remote(es.at[peer], buf_e.at[mult(me_y, YB), :], send_e.at[d - 1], recv_e.at[d - 1], "py", peer)

    def e_local():
        return pltpu.make_async_copy(es.at[me_y], buf_e.at[mult(me_y, YB), :], local_e.at[0])

    def c_copy(p, f, d):
        peer = other(me_s, d, S)
        return remote(buf_a.at[p, f, mult(peer, RY), :], buf_c.at[me_s, p, f],
                      send_c.at[p, f, d - 1], recv_c.at[p, f, d - 1], "snap", peer)

    def c_local(p):
        return pltpu.make_async_copy(buf_a.at[p, :, mult(me_s, RY), :], buf_c.at[me_s, p], local_c.at[p])

    def cy_copy(p, d):
        peer = other(me_s, d, S)
        return remote(buf_y.at[p, peer], buf_cy.at[me_s, p],
                      send_cy.at[p, d - 1], recv_cy.at[p, d - 1], "snap", peer)

    def cy_local(p):
        return pltpu.make_async_copy(buf_y.at[p, me_s], buf_cy.at[me_s, p], local_cy.at[p])

    def ce_copy(d):
        peer = other(me_s, d, S)
        return remote(buf_e.at[mult(peer, RY), :], buf_ce.at[me_s], send_ce.at[d - 1], recv_ce.at[d - 1], "snap", peer)

    def ce_local():
        return pltpu.make_async_copy(buf_e.at[mult(me_s, RY), :], buf_ce.at[me_s], local_ce.at[0])

    def b_rows(p):
        return pl.ds(pl.multiple_of((me_z * ZB + p) * 8, 8), 8)

    def b_copy(p, d):
        peer = other(me_z, d, PZ)
        return remote(buf_bs.at[p, peer], out.at[:, b_rows(p), :],
                      send_b.at[p, d - 1], recv_b.at[p, d - 1], "pz", peer)

    def b_local(p):
        return pltpu.make_async_copy(buf_bs.at[p, me_z], out.at[:, b_rows(p), :], local_b.at[p])

    barrier = pltpu.get_barrier_semaphore()
    for axis, me, n in (("py", me_y, PY), ("snap", me_s, S), ("pz", me_z, PZ)):
        for d in range(1, n):
            pl.semaphore_signal(barrier, inc=1, device_id={axis: other(me, d, n)}, device_id_type=MESH)
    pl.semaphore_wait(barrier, PY + S + PZ - 3)

    for p in range(ZB):
        for f in range(3):
            for d in range(1, PY):
                a_copy(p, f, d).start()
        a_local(p).start()
    planes_in = pltpu.make_async_copy(vel.at[0, 1:3], vw, local_v.at[0])
    planes_in.start()
    tables = [
        pltpu.make_async_copy(src, dst, local_t.at[t])
        for t, (src, dst) in enumerate(((gx_in, gx), (gy_in, gy), (tx_in, tx), (ty_in, ty), (gather_in, gather)))
    ]
    for table in tables:
        table.start()
    for r in range(RY):
        scale_y[r : r + 1, :] = jnp.full((1, XB), my[me_s * RY + r], F32)

    planes_in.wait()
    tables[0].wait()
    lane = lax.broadcasted_iota(jnp.int32, (YB, LANES), 1)
    for f in range(2):
        for p in range(ZB):
            j = 2 * p + f
            line = vw[f, p]
            ef[j] = dot(line, gx[0]) + dot(line, gx[1])
    for b in range(PY):
        total = jnp.zeros((YB, LANES), F32)
        for j in range(2 * ZB):
            shifted = pltpu.roll(ef[j], (NUMS * (j - b)) % LANES, 1)
            total = jnp.where((lane >= NUMS * j) & (lane < NUMS * (j + 1)), shifted, total)
        rounded = total.astype(BF16).astype(F32)
        low = (lane % NUMS == 5) | (lane % NUMS == 7)
        es[b] = jnp.where(low, total - rounded, rounded).astype(BF16)
    for d in range(1, PY):
        e_copy(d).start()
    e_local().start()

    tables[1].wait()

    def a_stage(p):
        a_local(p).wait()
        for f in range(3):
            for d in range(1, PY):
                a_copy(p, f, d).wait_recv()
            for d in range(1, S):
                c_copy(p, f, d).start()
        c_local(p).start()
        row = lax.broadcasted_iota(jnp.int32, (S * NUMS, XB), 0)
        low = (row % NUMS == 5) | (row % NUMS == 7)
        parts = []
        for f in (0, 2):
            field = buf_a[p, f]
            numbers = dot(gy[0], field) + dot(gy[1], field)
            rounded = numbers.astype(BF16).astype(F32)
            parts.append(jnp.where(low, numbers - rounded, rounded))
        for s in range(S):
            cut = slice(NUMS * s, NUMS * (s + 1))
            buf_y[p, s] = jnp.concatenate([parts[0][cut], parts[1][cut]], axis=0).astype(BF16)
        for d in range(1, S):
            cy_copy(p, d).start()
        cy_local(p).start()

    def e_stage():
        e_local().wait()
        for d in range(1, PY):
            e_copy(d).wait_recv()
        for d in range(1, S):
            ce_copy(d).start()
        ce_local().start()

    def se_stage():
        for table in tables[2:]:
            table.wait()
        ce_local().wait()
        for d in range(1, S):
            ce_copy(d).wait_recv()
        for k in range(K):
            total = sk[k, 0] * buf_ce[0].astype(F32)
            for s in range(1, S):
                total = total + sk[k, s] * buf_ce[s].astype(F32)
            se[RY * k : RY * (k + 1), :] = total

    def s_stage(p):
        c_local(p).wait()
        cy_local(p).wait()
        for d in range(1, S):
            for f in range(3):
                c_copy(p, f, d).wait_recv()
            cy_copy(p, d).wait_recv()

        def sketch(parts, k):
            total = sk[k, 0] * parts[0]
            for s in range(1, S):
                total = total + sk[k, s] * parts[s]
            return halves(total)

        for f in range(3):
            for t in range(RY // 16):
                rows = slice(16 * t, 16 * (t + 1))
                parts = [buf_c[s, p, f, rows, :].astype(F32) for s in range(S)]
                for k in range(K):
                    high, low = sketch(parts, k)
                    if f != 1:
                        yh[f // 2, rows, XB * k : XB * (k + 1)] = high
                        yl[f // 2, rows, XB * k : XB * (k + 1)] = low
                    own = slice(RY * k + 16 * t, RY * k + 16 * (t + 1))
                    if f != 0:
                        xh[f - 1, own, :XB] = high
                        xl[f - 1, own, :XB] = low
                    if f != 2:
                        pb[2 * f, own, :] = high
                        pb[2 * f + 1, own, :] = low
        parts = [buf_cy[s, p].astype(F32) for s in range(S)]
        for k in range(K):
            high, low = sketch(parts, k)
            for f in range(2):
                yh[f, RY : RY + 16, XB * k : XB * (k + 1)] = high
                yl[f, RY : RY + 16, XB * k : XB * (k + 1)] = low
        high, low = halves(pltpu.roll(se[...], lax.rem(LANES - 2 * NUMS * p, LANES), 1))
        for f in range(2):
            xh[f, :, XB:] = high
            xl[f, :, XB:] = low

        x_slopes = [dot(xh[f], tx[0, f]) + dot(xl[f], tx[0, f]) + dot(xh[f], tx[1, f]) for f in range(2)]
        y_slopes = [dot(ty[0, f], yh[f]) + dot(ty[0, f], yl[f]) + dot(ty[1, f], yh[f]) for f in range(2)]
        scale_x = mx[0:1, mult(me_y, XB)]
        for k in range(K):
            own, cols = slice(RY * k, RY * (k + 1)), slice(XB * k, XB * (k + 1))
            pb[4, own, :] = (x_slopes[1][own] * scale_x).astype(BF16)
            pb[5, own, :] = (y_slopes[1][:, cols] * scale_y[...]).astype(BF16)
            pb[6, own, :] = (x_slopes[0][own] * scale_x - y_slopes[0][:, cols] * scale_y[...]).astype(BF16)
        for f in range(fields):
            moved = dot(gather[...], pb[f]).astype(BF16)
            for q in range(PZ):
                for g in range(groups):
                    cut = (q * groups + g) * 8
                    buf_bs[p, q, g * fields + f] = moved[cut : cut + 8]
        for d in range(1, PZ):
            b_copy(p, d).start()
        b_local(p).start()

    lag = min(3, ZB)

    @pl.loop(0, ZB + lag)
    def _(i):
        @pl.when(i < ZB)
        def _():
            a_stage(i)

        @pl.when(i == 1)
        def _():
            e_stage()

        @pl.when(i == lag)
        def _():
            se_stage()

        @pl.when(i >= lag)
        def _():
            s_stage(i - lag)

    for p in range(ZB):
        b_local(p).wait()
        for d in range(1, PZ):
            b_copy(p, d).wait_recv()

    for p in range(ZB):
        for f in range(3):
            for d in range(1, PY):
                a_copy(p, f, d).wait_send()
            for d in range(1, S):
                c_copy(p, f, d).wait_send()
        for d in range(1, S):
            cy_copy(p, d).wait_send()
        for d in range(1, PZ):
            b_copy(p, d).wait_send()
    for d in range(1, PY):
        e_copy(d).wait_send()
    for d in range(1, S):
        ce_copy(d).wait_send()


def z_body(z, lines, dz, turn, mz, out):
    K, NZ, XB = z["K"], z["NZ"], z["XB"]
    same = lax.broadcasted_iota(jnp.int32, (NZ, NZ), 0) == lax.broadcasted_iota(jnp.int32, (NZ, NZ), 1)
    scale_z = jnp.broadcast_to(jnp.sum(jnp.where(same, mz[...], 0.0), axis=1, keepdims=True), (NZ, XB))
    slope = [dot(dz[0], lines[2 * f]) + dot(dz[0], lines[2 * f + 1]) + dot(dz[1], lines[2 * f]) for f in range(2)]
    w_x, w_y, spin_z = (dot(turn[...], lines[f]) for f in (4, 5, 6))
    for i in range(8):
        r, k = divmod(i, K)
        cut = slice(NZ * i, NZ * (i + 1))
        out[k, 0, r] = w_y[cut] - slope[1][cut] * scale_z
        out[k, 1, r] = slope[0][cut] * scale_z - w_x[cut]
        out[k, 2, r] = spin_z[cut]


def solution(mesh):
    def step(velocity, metric_x, metric_y, metric_z, sketch_matrix):
        whole = (1, 3, velocity.shape[2] * mesh.shape["pz"], velocity.shape[3] * mesh.shape["py"], velocity.shape[4])
        z = sizes_of(mesh, whole, sketch_matrix.shape[1])
        S, PY, PZ, K, ZB, YB, XB, RY, RG, NX, NY, NZ = (z[n] for n in (
            "S", "PY", "PZ", "K", "ZB", "YB", "XB", "RY", "RG", "NX", "NY", "NZ"))
        tables, z_tables = tables_of(z)
        groups, fields = K * RG // 8, 7
        dma = pltpu.SemaphoreType.DMA
        vmem, anywhere = pl.BlockSpec(memory_space=pltpu.VMEM), pl.BlockSpec(memory_space=pl.ANY)
        lines = pl.pallas_call(
            functools.partial(body, z),
            out_shape=jax.ShapeDtypeStruct((groups * fields, 8 * NZ, XB), BF16),
            in_specs=[anywhere] * 6 + [vmem] + [pl.BlockSpec(memory_space=pltpu.SMEM)] * 2,
            out_specs=anywhere,
            scratch_shapes=[pltpu.VMEM(t.shape, t.dtype) for t in tables] + [
                pltpu.VMEM((RY, XB), F32),
                pltpu.VMEM((2, ZB, YB, NX), BF16),
                pltpu.VMEM((2 * ZB, YB, LANES), F32),
                pltpu.VMEM((PY, YB, LANES), BF16),
                pltpu.VMEM((ZB, 3, NY, XB), BF16),
                pltpu.VMEM((NY, LANES), BF16),
                pltpu.VMEM((ZB, S, 16, XB), BF16),
                pltpu.VMEM((S, ZB, 3, RY, XB), BF16),
                pltpu.VMEM((S, ZB, 16, XB), BF16),
                pltpu.VMEM((S, RY, LANES), BF16),
                pltpu.VMEM((K * RY, LANES), F32),
                pltpu.VMEM((2, K * RY, XB + LANES), BF16),
                pltpu.VMEM((2, K * RY, XB + LANES), BF16),
                pltpu.VMEM((2, RY + 16, K * XB), BF16),
                pltpu.VMEM((2, RY + 16, K * XB), BF16),
                pltpu.VMEM((fields, K * RY, XB), BF16),
                pltpu.VMEM((ZB, PZ, groups * fields, 8, XB), BF16),
                dma((ZB, 3, PY - 1)), dma((ZB, 3, PY - 1)), dma((PY - 1,)), dma((PY - 1,)),
                dma((ZB, 3, S - 1)), dma((ZB, 3, S - 1)), dma((ZB, S - 1)), dma((ZB, S - 1)),
                dma((S - 1,)), dma((S - 1,)), dma((ZB, PZ - 1)), dma((ZB, PZ - 1)),
                dma((5,)), dma((1,)), dma((ZB,)), dma((1,)), dma((ZB,)), dma((ZB,)), dma((1,)), dma((ZB,)),
            ],
            compiler_params=pltpu.CompilerParams(
                collective_id=0, has_side_effects=True, vmem_limit_bytes=56 * 1024 * 1024),
        )(velocity, *tables, metric_x[None, :], metric_y, sketch_matrix.T)
        per = 8 // K
        whole_block = lambda t: pl.BlockSpec(t.shape, lambda g: (0,) * t.ndim)
        metric_row = metric_z[None, :]
        result = pl.pallas_call(
            functools.partial(z_body, z),
            grid=(groups,),
            out_shape=jax.ShapeDtypeStruct((K, 3, RG, NZ, XB), F32),
            in_specs=[pl.BlockSpec((fields, 8 * NZ, XB), lambda g: (g, 0, 0))] + [whole_block(t) for t in (*z_tables, metric_row)],
            out_specs=pl.BlockSpec((K, 3, per, NZ, XB), lambda g: (0, 0, g, 0, 0)),
        )(lines, *z_tables, metric_row)
        return jnp.swapaxes(result, 2, 3)

    return jax.shard_map(
        step,
        mesh=mesh,
        in_specs=(P("snap", None, "pz", "py", None), P(), P(), P(), P()),
        out_specs=P(None, None, None, ("snap", "pz"), "py"),
        check_vma=False,
    )
```

```python
import functools

import jax
import jax.numpy as jnp
import numpy as np
from jax import lax
from jax.experimental import pallas as pl
from jax.experimental.pallas import tpu as pltpu
from jax.sharding import PartitionSpec as P

MESH = pl.DeviceIdType.MESH
F32 = jnp.float32
BF16 = jnp.bfloat16
LANES = 128
NUMS = 4


def tridiagonal(n):
    return np.eye(n) + (np.eye(n, k=1) + np.eye(n, k=-1)) / 3.0


def right_side(n):
    first = np.eye(n, k=1) - np.eye(n, k=-1)
    second = np.eye(n, k=2) - np.eye(n, k=-2)
    return 7.0 / 9.0 * first + 1.0 / 36.0 * second


def derivative(n):
    return np.linalg.solve(tridiagonal(n), right_side(n))


def block_table(n):
    halo = np.zeros((n, NUMS))
    edge = 7.0 / 9.0 + 1.0 / 36.0
    halo[0, 0], halo[1, 0], halo[0, 1] = -edge, -1.0 / 36.0, 1.0
    halo[n - 1, 2], halo[n - 2, 2], halo[n - 1, 3] = edge, 1.0 / 36.0, 1.0
    return np.linalg.solve(tridiagonal(n), np.concatenate([right_side(n), halo], axis=1))


def interface_rows(n, blocks):
    whole, size = derivative(n), n // blocks
    rows = np.zeros((blocks, NUMS, n))
    for block in range(blocks):
        low, high = block * size, (block + 1) * size
        if block > 0:
            rows[block, 0, low - 1] = 1.0
            rows[block, 1] = -whole[low - 1] / 3.0
            rows[block, 1, low - 1] += 1.0 / 36.0
            rows[block, 1, low - 2] -= 1.0 / 36.0
        if block < blocks - 1:
            rows[block, 2, high] = 1.0
            rows[block, 3] = -whole[high] / 3.0
            rows[block, 3, high + 1] += 1.0 / 36.0
            rows[block, 3, high] -= 1.0 / 36.0
    return rows.reshape(blocks * NUMS, n)


def split(table):
    high = np.asarray(table, np.float32).astype(BF16)
    low = (np.asarray(table, np.float64) - high.astype(np.float64)).astype(BF16)
    return np.stack([high, low])


def dot(left, right):
    return jnp.dot(left, right, preferred_element_type=F32)


def halves(value):
    high = value.astype(BF16)
    return high, (value - high.astype(F32)).astype(BF16)


def sizes_of(mesh, shape, rank):
    snaps, nyblocks, nzblocks = mesh.shape["snap"], mesh.shape["py"], mesh.shape["pz"]
    nz, ny, nx = shape[2:]
    return dict(
        S=snaps, PY=nyblocks, PZ=nzblocks, K=rank, ZB=nz // nzblocks, YB=ny // nyblocks,
        XB=nx // nyblocks, RY=ny // snaps, RG=ny // snaps // nzblocks, NX=nx, NY=ny, NZ=nz,
    )


def tables_of(z):
    S, PY, PZ, K, RY, RG, XB, NZ = (z[n] for n in ("S", "PY", "PZ", "K", "RY", "RG", "XB", "NZ"))
    gx = np.zeros((z["NX"], LANES))
    gx[:, : PY * NUMS] = interface_rows(z["NX"], PY).T
    numbers_y = interface_rows(z["NY"], S).reshape(S, NUMS, z["NY"])
    gy = np.zeros((2, S, 2, NUMS, z["NY"]))
    gy[0, :, 0] = gy[1, :, 1] = numbers_y
    gy = gy.reshape(2, 2 * NUMS * S, z["NY"])
    bx, by = block_table(XB), block_table(RY)
    tx = np.zeros((2, XB + LANES, XB))
    ty = np.zeros((2, RY, RY + 16))
    for f in range(2):
        tx[f, :XB] = bx[:, :XB].T
        tx[f, XB + NUMS * f : XB + NUMS * (f + 1)] = bx[:, XB:].T
        ty[f, :, :RY] = by[:, :RY]
        ty[f, :, RY + NUMS * f : RY + NUMS * (f + 1)] = by[:, RY:]
    dz = np.einsum("zw,ij->izwj", derivative(NZ), np.eye(8)).reshape(8 * NZ, 8 * NZ)
    turn = np.einsum("zw,ij->izwj", np.eye(NZ), np.eye(8)).reshape(8 * NZ, 8 * NZ)
    gather = np.zeros((K * RY, K * RY))
    groups = K * RG // 8
    for k in range(K):
        for q in range(PZ):
            for r in range(RG):
                g, i = divmod(r * K + k, 8)
                gather[(q * groups + g) * 8 + i, k * RY + q * RG + r] = 1.0
    one = lambda t: jnp.asarray(t.astype(np.float32)).astype(BF16)
    return [jnp.asarray(split(t)) for t in (gx, gy, tx, ty)] + [one(gather)], [jnp.asarray(split(dz)), one(turn)]


def body(
    z, vel, gx_in, gy_in, tx_in, ty_in, gather_in, mx_in, my_in, sk_in, out,
    gx, gy, tx, ty, gather, mx, my, sk, scale_y,
    vw, ef, es, buf_a, buf_e, buf_y, buf_c, buf_cy, buf_ce, se, xh, xl, yh, yl, pb, buf_bs,
    send_a, recv_a, send_e, recv_e, send_c, recv_c, send_cy, recv_cy, send_ce, recv_ce, send_b, recv_b,
    local_t, local_v, local_a, local_e, local_c, local_cy, local_ce, local_b,
):
    S, PY, PZ, K, ZB, YB, XB, RY, RG = (z[n] for n in ("S", "PY", "PZ", "K", "ZB", "YB", "XB", "RY", "RG"))
    groups, fields = K * RG // 8, 7
    me_s, me_y, me_z = lax.axis_index("snap"), lax.axis_index("py"), lax.axis_index("pz")

    def other(me, d, n):
        return lax.rem(me + d, n)

    def remote(src, dst, send, recv, axis, peer):
        return pltpu.make_async_remote_copy(
            src_ref=src, dst_ref=dst, send_sem=send, recv_sem=recv, device_id={axis: peer}, device_id_type=MESH)

    def mult(value, size):
        return pl.ds(pl.multiple_of(value * size, size), size)

    def a_copy(p, f, d):
        peer = other(me_y, d, PY)
        return remote(vel.at[0, f, p, :, mult(peer, XB)], buf_a.at[p, f, mult(me_y, YB), :],
                      send_a.at[p, f, d - 1], recv_a.at[p, f, d - 1], "py", peer)

    def a_local(p):
        return pltpu.make_async_copy(vel.at[0, :, p, :, mult(me_y, XB)], buf_a.at[p, :, mult(me_y, YB), :], local_a.at[p])

    def e_copy(d):
        peer = other(me_y, d, PY)
        return remote(es.at[peer], buf_e.at[mult(me_y, YB), :], send_e.at[d - 1], recv_e.at[d - 1], "py", peer)

    def e_local():
        return pltpu.make_async_copy(es.at[me_y], buf_e.at[mult(me_y, YB), :], local_e.at[0])

    def c_copy(p, f, d):
        peer = other(me_s, d, S)
        return remote(buf_a.at[p, f, mult(peer, RY), :], buf_c.at[me_s, p, f],
                      send_c.at[p, f, d - 1], recv_c.at[p, f, d - 1], "snap", peer)

    def c_local(p):
        return pltpu.make_async_copy(buf_a.at[p, :, mult(me_s, RY), :], buf_c.at[me_s, p], local_c.at[p])

    def cy_copy(p, d):
        peer = other(me_s, d, S)
        return remote(buf_y.at[p, peer], buf_cy.at[me_s, p],
                      send_cy.at[p, d - 1], recv_cy.at[p, d - 1], "snap", peer)

    def cy_local(p):
        return pltpu.make_async_copy(buf_y.at[p, me_s], buf_cy.at[me_s, p], local_cy.at[p])

    def ce_copy(d):
        peer = other(me_s, d, S)
        return remote(buf_e.at[mult(peer, RY), :], buf_ce.at[me_s], send_ce.at[d - 1], recv_ce.at[d - 1], "snap", peer)

    def ce_local():
        return pltpu.make_async_copy(buf_e.at[mult(me_s, RY), :], buf_ce.at[me_s], local_ce.at[0])

    def b_rows(p):
        return pl.ds(pl.multiple_of((me_z * ZB + p) * 8, 8), 8)

    part_of = (slice(0, 5), slice(5, 7))

    def b_copy(p, part, d):
        peer = other(me_z, d, PZ)
        return remote(buf_bs.at[p, peer, part_of[part]], out.at[part_of[part], :, b_rows(p), :],
                      send_b.at[p, part, d - 1], recv_b.at[p, part, d - 1], "pz", peer)

    def b_local(p, part):
        return pltpu.make_async_copy(
            buf_bs.at[p, me_z, part_of[part]], out.at[part_of[part], :, b_rows(p), :], local_b.at[p, part])

    barrier = pltpu.get_barrier_semaphore()
    for axis, me, n in (("py", me_y, PY), ("snap", me_s, S), ("pz", me_z, PZ)):
        for d in range(1, n):
            pl.semaphore_signal(barrier, inc=1, device_id={axis: other(me, d, n)}, device_id_type=MESH)
    pl.semaphore_wait(barrier, PY + S + PZ - 3)

    def a_start(p):
        for f in range(3):
            for d in range(1, PY):
                a_copy(p, f, d).start()
        a_local(p).start()

    lag = min(3, ZB)
    for p in range(lag):
        a_start(p)
    planes_in = pltpu.make_async_copy(vel.at[0, 1:3], vw, local_v.at[0])
    planes_in.start()
    pairs = ((gx_in, gx), (my_in, my), (gy_in, gy), (sk_in, sk), (tx_in, tx), (ty_in, ty), (gather_in, gather),
             (mx_in.at[:, mult(me_y, XB)], mx))
    tables = [pltpu.make_async_copy(src, dst, local_t.at[t]) for t, (src, dst) in enumerate(pairs)]
    for table in tables:
        table.start()
    for part in (yh, yl):
        part[:, RY + 2 * NUMS :, :] = jnp.zeros((2, 16 - 2 * NUMS, K * XB), BF16)

    planes_in.wait()
    tables[0].wait()
    lane = lax.broadcasted_iota(jnp.int32, (YB, LANES), 1)
    for f in range(2):
        for p in range(ZB):
            j = 2 * p + f
            line = vw[f, p]
            ef[j] = dot(line, gx[0]) + dot(line, gx[1])
    for b in range(PY):
        total = jnp.zeros((YB, LANES), F32)
        for j in range(2 * ZB):
            shifted = pltpu.roll(ef[j], (NUMS * (j - b)) % LANES, 1)
            total = jnp.where((lane >= NUMS * j) & (lane < NUMS * (j + 1)), shifted, total)
        es[b] = total.astype(BF16)
    for d in range(1, PY):
        e_copy(d).start()
    e_local().start()

    for p in range(lag, ZB):
        a_start(p)
    tables[1].wait()
    for r in range(RY):
        scale_y[r : r + 1, :] = jnp.full((1, XB), my[me_s * RY + r], F32)
    tables[2].wait()

    def a_stage(p):
        a_local(p).wait()
        for f in range(3):
            for d in range(1, PY):
                a_copy(p, f, d).wait_recv()
            if f < 2:
                for d in range(1, S):
                    c_copy(p, f, d).start()
        numbers = (dot(gy[0, 0], buf_a[p, 0]) + dot(gy[1, 0], buf_a[p, 0])) + (
            dot(gy[0, 1], buf_a[p, 2]) + dot(gy[1, 1], buf_a[p, 2]))
        for s in range(S):
            buf_y[p, s] = numbers[2 * NUMS * s : 2 * NUMS * (s + 1)].astype(BF16)
        for d in range(1, S):
            cy_copy(p, d).start()
        for d in range(1, S):
            c_copy(p, 2, d).start()
        c_local(p).start()
        cy_local(p).start()

    def e_stage():
        e_local().wait()
        for d in range(1, PY):
            e_copy(d).wait_recv()
        for d in range(1, S):
            ce_copy(d).start()
        ce_local().start()

    def se_stage():
        for table in tables[3:]:
            table.wait()
        ce_local().wait()
        for d in range(1, S):
            ce_copy(d).wait_recv()
        for k in range(K):
            total = sk[k, 0] * buf_ce[0].astype(F32)
            for s in range(1, S):
                total = total + sk[k, s] * buf_ce[s].astype(F32)
            se[RY * k : RY * (k + 1), :] = total

    def sketch(parts, k):
        total = sk[k, 0] * parts[0]
        for s in range(1, S):
            total = total + sk[k, s] * parts[s]
        return halves(total)

    def sketch_field(p, f):
        for t in range(RY // 16):
            rows = slice(16 * t, 16 * (t + 1))
            parts = [buf_c[s, p, f, rows, :].astype(F32) for s in range(S)]
            for k in range(K):
                high, low = sketch(parts, k)
                own = slice(RY * k + 16 * t, RY * k + 16 * (t + 1))
                if f != 1:
                    yh[f // 2, rows, XB * k : XB * (k + 1)] = high
                    yl[f // 2, rows, XB * k : XB * (k + 1)] = low
                if f != 0:
                    xh[f - 1, own, :XB] = high
                    xl[f - 1, own, :XB] = low
                if f != 2:
                    pb[2 * f, own, :] = high
                    pb[2 * f + 1, own, :] = low

    def x_slope(f):
        return dot(xh[f], tx[0, f]) + dot(xl[f], tx[0, f]) + dot(xh[f], tx[1, f])

    def y_slope(f):
        return dot(ty[0, f], yh[f]) + dot(ty[0, f], yl[f]) + dot(ty[1, f], yh[f])

    def send_part(p, part):
        for f in range(part_of[part].start, part_of[part].stop):
            moved = dot(gather[...], pb[f]).astype(BF16)
            for q in range(PZ):
                for g in range(groups):
                    cut = (q * groups + g) * 8
                    buf_bs[p, q, f, g] = moved[cut : cut + 8]
        for d in range(1, PZ):
            b_copy(p, part, d).start()
        b_local(p, part).start()

    def s_stage(p):
        c_local(p).wait()
        cy_local(p).wait()
        for d in range(1, S):
            c_copy(p, 0, d).wait_recv()
            c_copy(p, 1, d).wait_recv()
            cy_copy(p, d).wait_recv()
        sketch_field(p, 0)
        sketch_field(p, 1)
        parts = [buf_cy[s, p].astype(F32) for s in range(S)]
        for k in range(K):
            high, low = sketch(parts, k)
            for f in range(2):
                yh[f, RY : RY + 2 * NUMS, XB * k : XB * (k + 1)] = high
                yl[f, RY : RY + 2 * NUMS, XB * k : XB * (k + 1)] = low
        high, low = halves(pltpu.roll(se[...], lax.rem(LANES - 2 * NUMS * p, LANES), 1))
        for f in range(2):
            xh[f, :, XB:] = high
            xl[f, :, XB:] = low
        scale_x = mx[...]
        x_slopes, y_slopes = x_slope(0), y_slope(0)
        for k in range(K):
            own, cols = slice(RY * k, RY * (k + 1)), slice(XB * k, XB * (k + 1))
            pb[4, own, :] = (x_slopes[own] * scale_x - y_slopes[:, cols] * scale_y[...]).astype(BF16)
        send_part(p, 0)

        for d in range(1, S):
            c_copy(p, 2, d).wait_recv()
        sketch_field(p, 2)
        x_slopes, y_slopes = x_slope(1), y_slope(1)
        for k in range(K):
            own, cols = slice(RY * k, RY * (k + 1)), slice(XB * k, XB * (k + 1))
            pb[5, own, :] = (x_slopes[own] * scale_x).astype(BF16)
            pb[6, own, :] = (y_slopes[:, cols] * scale_y[...]).astype(BF16)
        send_part(p, 1)

    @pl.loop(0, ZB + lag)
    def _(i):
        @pl.when(i < ZB)
        def _():
            a_stage(i)

        @pl.when(i == lag - 1)
        def _():
            e_stage()

        @pl.when(i == lag)
        def _():
            se_stage()

        @pl.when(i >= lag)
        def _():
            s_stage(i - lag)

    for p in range(ZB):
        for part in range(2):
            b_local(p, part).wait()
            for d in range(1, PZ):
                b_copy(p, part, d).wait_recv()

    for p in range(ZB):
        for f in range(3):
            for d in range(1, PY):
                a_copy(p, f, d).wait_send()
            for d in range(1, S):
                c_copy(p, f, d).wait_send()
        for d in range(1, S):
            cy_copy(p, d).wait_send()
        for part in range(2):
            for d in range(1, PZ):
                b_copy(p, part, d).wait_send()
    for d in range(1, PY):
        e_copy(d).wait_send()
    for d in range(1, S):
        ce_copy(d).wait_send()


def z_body(z, lines, dz, turn, mz, out):
    K, NZ, XB = z["K"], z["NZ"], z["XB"]
    same = lax.broadcasted_iota(jnp.int32, (NZ, NZ), 0) == lax.broadcasted_iota(jnp.int32, (NZ, NZ), 1)
    scale_z = jnp.broadcast_to(jnp.sum(jnp.where(same, mz[...], 0.0), axis=1, keepdims=True), (NZ, XB))
    slope = [dot(dz[0], lines[2 * f]) + dot(dz[0], lines[2 * f + 1]) + dot(dz[1], lines[2 * f]) for f in range(2)]
    w_x, w_y, spin_z = (dot(turn[...], lines[f]) for f in (5, 6, 4))
    for i in range(8):
        r, k = divmod(i, K)
        cut = slice(NZ * i, NZ * (i + 1))
        out[k, 0, r] = w_y[cut] - slope[1][cut] * scale_z
        out[k, 1, r] = slope[0][cut] * scale_z - w_x[cut]
        out[k, 2, r] = spin_z[cut]


def solution(mesh):
    def step(velocity, metric_x, metric_y, metric_z, sketch_matrix):
        whole = (1, 3, velocity.shape[2] * mesh.shape["pz"], velocity.shape[3] * mesh.shape["py"], velocity.shape[4])
        z = sizes_of(mesh, whole, sketch_matrix.shape[1])
        S, PY, PZ, K, ZB, YB, XB, RY, RG, NX, NY, NZ = (z[n] for n in (
            "S", "PY", "PZ", "K", "ZB", "YB", "XB", "RY", "RG", "NX", "NY", "NZ"))
        tables, z_tables = tables_of(z)
        groups, fields = K * RG // 8, 7
        dma = pltpu.SemaphoreType.DMA
        anywhere = pl.BlockSpec(memory_space=pl.ANY)
        lines = pl.pallas_call(
            functools.partial(body, z),
            out_shape=jax.ShapeDtypeStruct((fields, groups, 8 * NZ, XB), BF16),
            in_specs=[anywhere] * 9,
            out_specs=anywhere,
            scratch_shapes=[pltpu.VMEM(t.shape, t.dtype) for t in tables] + [
                pltpu.VMEM((1, XB), F32),
                pltpu.SMEM((NY,), F32),
                pltpu.SMEM((K, S), F32),
                pltpu.VMEM((RY, XB), F32),
                pltpu.VMEM((2, ZB, YB, NX), BF16),
                pltpu.VMEM((2 * ZB, YB, LANES), F32),
                pltpu.VMEM((PY, YB, LANES), BF16),
                pltpu.VMEM((ZB, 3, NY, XB), BF16),
                pltpu.VMEM((NY, LANES), BF16),
                pltpu.VMEM((ZB, S, 2 * NUMS, XB), BF16),
                pltpu.VMEM((S, ZB, 3, RY, XB), BF16),
                pltpu.VMEM((S, ZB, 2 * NUMS, XB), BF16),
                pltpu.VMEM((S, RY, LANES), BF16),
                pltpu.VMEM((K * RY, LANES), F32),
                pltpu.VMEM((2, K * RY, XB + LANES), BF16),
                pltpu.VMEM((2, K * RY, XB + LANES), BF16),
                pltpu.VMEM((2, RY + 16, K * XB), BF16),
                pltpu.VMEM((2, RY + 16, K * XB), BF16),
                pltpu.VMEM((fields, K * RY, XB), BF16),
                pltpu.VMEM((ZB, PZ, fields, groups, 8, XB), BF16),
                dma((ZB, 3, PY - 1)), dma((ZB, 3, PY - 1)), dma((PY - 1,)), dma((PY - 1,)),
                dma((ZB, 3, S - 1)), dma((ZB, 3, S - 1)), dma((ZB, S - 1)), dma((ZB, S - 1)),
                dma((S - 1,)), dma((S - 1,)), dma((ZB, 2, PZ - 1)), dma((ZB, 2, PZ - 1)),
                dma((8,)), dma((1,)), dma((ZB,)), dma((1,)), dma((ZB,)), dma((ZB,)), dma((1,)), dma((ZB, 2)),
            ],
            compiler_params=pltpu.CompilerParams(
                collective_id=0, has_side_effects=True, vmem_limit_bytes=56 * 1024 * 1024),
        )(velocity, *tables, metric_x[None, :], metric_y, sketch_matrix.T)
        per = 8 // K
        whole_block = lambda t: pl.BlockSpec(t.shape, lambda g: (0,) * t.ndim)
        metric_row = metric_z[None, :]
        result = pl.pallas_call(
            functools.partial(z_body, z),
            grid=(groups,),
            out_shape=jax.ShapeDtypeStruct((K, 3, RG, NZ, XB), F32),
            in_specs=[pl.BlockSpec((fields, pl.Squeezed(), 8 * NZ, XB), lambda g: (0, g, 0, 0))] + [whole_block(t) for t in (*z_tables, metric_row)],
            out_specs=pl.BlockSpec((K, 3, per, NZ, XB), lambda g: (0, 0, g, 0, 0)),
        )(lines, *z_tables, metric_row)
        return jnp.swapaxes(result, 2, 3)

    return jax.shard_map(
        step,
        mesh=mesh,
        in_specs=(P("snap", None, "pz", "py", None), P(), P(), P(), P()),
        out_specs=P(None, None, None, ("snap", "pz"), "py"),
        check_vma=False,
    )
```

```python
import functools

import jax
import jax.numpy as jnp
import numpy as np
from jax import lax
from jax.experimental import pallas as pl
from jax.experimental.pallas import tpu as pltpu
from jax.sharding import PartitionSpec as P

MESH = pl.DeviceIdType.MESH
F32 = jnp.float32
BF16 = jnp.bfloat16
LANES = 128
NUMS = 4


def tridiagonal(n):
    return np.eye(n) + (np.eye(n, k=1) + np.eye(n, k=-1)) / 3.0


def right_side(n):
    first = np.eye(n, k=1) - np.eye(n, k=-1)
    second = np.eye(n, k=2) - np.eye(n, k=-2)
    return 7.0 / 9.0 * first + 1.0 / 36.0 * second


def derivative(n):
    return np.linalg.solve(tridiagonal(n), right_side(n))


def block_table(n):
    halo = np.zeros((n, NUMS))
    edge = 7.0 / 9.0 + 1.0 / 36.0
    halo[0, 0], halo[1, 0], halo[0, 1] = -edge, -1.0 / 36.0, 1.0
    halo[n - 1, 2], halo[n - 2, 2], halo[n - 1, 3] = edge, 1.0 / 36.0, 1.0
    return np.linalg.solve(tridiagonal(n), np.concatenate([right_side(n), halo], axis=1))


def interface_rows(n, blocks):
    whole, size = derivative(n), n // blocks
    rows = np.zeros((blocks, NUMS, n))
    for block in range(blocks):
        low, high = block * size, (block + 1) * size
        if block > 0:
            rows[block, 0, low - 1] = 1.0
            rows[block, 1] = -whole[low - 1] / 3.0
            rows[block, 1, low - 1] += 1.0 / 36.0
            rows[block, 1, low - 2] -= 1.0 / 36.0
        if block < blocks - 1:
            rows[block, 2, high] = 1.0
            rows[block, 3] = -whole[high] / 3.0
            rows[block, 3, high + 1] += 1.0 / 36.0
            rows[block, 3, high] -= 1.0 / 36.0
    return rows.reshape(blocks * NUMS, n)


def split(table):
    high = np.asarray(table, np.float32).astype(BF16)
    low = (np.asarray(table, np.float64) - high.astype(np.float64)).astype(BF16)
    return np.stack([high, low])


def dot(left, right):
    return jnp.dot(left, right, preferred_element_type=F32)


def halves(value):
    high = value.astype(BF16)
    return high, (value - high.astype(F32)).astype(BF16)


def far_first(n):
    return sorted(range(1, n), key=lambda d: -min(d, n - d))


def sizes_of(mesh, shape, rank):
    snaps, nyblocks, nzblocks = mesh.shape["snap"], mesh.shape["py"], mesh.shape["pz"]
    nz, ny, nx = shape[2:]
    return dict(
        S=snaps, PY=nyblocks, PZ=nzblocks, K=rank, ZB=nz // nzblocks, YB=ny // nyblocks,
        XB=nx // nyblocks, RY=ny // snaps, RG=ny // snaps // nzblocks, NX=nx, NY=ny, NZ=nz,
    )


def tables_of(z):
    S, PY, PZ, K, RY, RG, XB, NZ = (z[n] for n in ("S", "PY", "PZ", "K", "RY", "RG", "XB", "NZ"))
    gx = np.zeros((z["NX"], LANES))
    gx[:, : PY * NUMS] = interface_rows(z["NX"], PY).T
    numbers_y = interface_rows(z["NY"], S).reshape(S, NUMS, z["NY"])
    gy = np.zeros((2, S, 2, NUMS, z["NY"]))
    gy[0, :, 0] = gy[1, :, 1] = numbers_y
    gy = gy.reshape(2, 2 * NUMS * S, z["NY"])
    bx, by = block_table(XB), block_table(RY)
    tx = np.zeros((2, XB + LANES, XB))
    ty = np.zeros((2, RY, RY + 16))
    for f in range(2):
        tx[f, :XB] = bx[:, :XB].T
        tx[f, XB + NUMS * f : XB + NUMS * (f + 1)] = bx[:, XB:].T
        ty[f, :, :RY] = by[:, :RY]
        ty[f, :, RY + NUMS * f : RY + NUMS * (f + 1)] = by[:, RY:]
    dz = np.einsum("zw,ij->izwj", derivative(NZ), np.eye(8)).reshape(8 * NZ, 8 * NZ)
    turn = np.einsum("zw,ij->izwj", np.eye(NZ), np.eye(8)).reshape(8 * NZ, 8 * NZ)
    gather = np.zeros((K * RY, K * RY))
    groups = K * RG // 8
    for k in range(K):
        for q in range(PZ):
            for r in range(RG):
                g, i = divmod(r * K + k, 8)
                gather[(q * groups + g) * 8 + i, k * RY + q * RG + r] = 1.0
    one = lambda t: jnp.asarray(t.astype(np.float32)).astype(BF16)
    return [jnp.asarray(split(t)) for t in (gx, gy, tx, ty)] + [one(gather)], [jnp.asarray(split(dz)), one(turn)]


def body(
    z, vel, gx_in, gy_in, tx_in, ty_in, gather_in, mx_in, my_in, sk_in, out,
    gx, gy, tx, ty, gather, mx, my, sk, scale_y,
    vw, ef, es, buf_a, buf_v, buf_e, buf_c, buf_cv, buf_ce, se, xh, xl, yh, yl, pb, buf_bs,
    send_a, recv_a, send_e, recv_e, send_c, recv_c, send_ce, recv_ce, send_b, recv_b,
    local_t, local_v, local_a, local_e, local_c, local_ce, local_b,
):
    S, PY, PZ, K, ZB, YB, XB, RY, RG = (z[n] for n in ("S", "PY", "PZ", "K", "ZB", "YB", "XB", "RY", "RG"))
    groups, H = K * RG // 8, YB // RY
    me_s, me_y, me_z = lax.axis_index("snap"), lax.axis_index("py"), lax.axis_index("pz")

    def other(me, d, n):
        return lax.rem(me + d, n)

    def remote(src, dst, send, recv, axis, peer):
        return pltpu.make_async_remote_copy(
            src_ref=src, dst_ref=dst, send_sem=send, recv_sem=recv, device_id={axis: peer}, device_id_type=MESH)

    def mult(value, size):
        return pl.ds(pl.multiple_of(value * size, size), size)

    def a_ends(p, f, peer):
        own = pl.ds(me_y * H, H)
        dst = buf_v.at[p, own, :RY, :] if f == 1 else buf_a.at[p, f // 2, own]
        return vel.at[0, f, p, :, :, mult(peer, XB)], dst

    def a_copy(p, f, d):
        peer = other(me_y, d, PY)
        return remote(*a_ends(p, f, peer), send_a.at[p, f, d - 1], recv_a.at[p, f, d - 1], "py", peer)

    def a_local(p, f):
        return pltpu.make_async_copy(*a_ends(p, f, me_y), local_a.at[p, f])

    def e_copy(d):
        peer = other(me_y, d, PY)
        return remote(es.at[peer], buf_e.at[mult(me_y, YB // 2), :], send_e.at[d - 1], recv_e.at[d - 1], "py", peer)

    def e_local():
        return pltpu.make_async_copy(es.at[me_y], buf_e.at[mult(me_y, YB // 2), :], local_e.at[0])

    def c_ends(p, f, peer):
        if f == 1:
            return buf_v.at[p, peer], buf_cv.at[me_s, p]
        return buf_a.at[p, f // 2, peer], buf_c.at[me_s, p, f // 2]

    def c_copy(p, f, d):
        peer = other(me_s, d, S)
        return remote(*c_ends(p, f, peer), send_c.at[p, f, d - 1], recv_c.at[p, f, d - 1], "snap", peer)

    def c_local(p, f):
        return pltpu.make_async_copy(*c_ends(p, f, me_s), local_c.at[p, f])

    def ce_copy(d):
        peer = other(me_s, d, S)
        return remote(buf_e.at[mult(peer, RY // 2), :], buf_ce.at[me_s], send_ce.at[d - 1], recv_ce.at[d - 1], "snap", peer)

    def ce_local():
        return pltpu.make_async_copy(buf_e.at[mult(me_s, RY // 2), :], buf_ce.at[me_s], local_ce.at[0])

    def b_rows(p):
        return pl.ds(pl.multiple_of((me_z * ZB + p) * 8, 8), 8)

    part_of = (slice(0, 5), slice(5, 7))

    def b_copy(p, part, d):
        peer = other(me_z, d, PZ)
        return remote(buf_bs.at[p, peer, part_of[part]], out.at[part_of[part], :, b_rows(p), :],
                      send_b.at[p, part, d - 1], recv_b.at[p, part, d - 1], "pz", peer)

    def b_local(p, part):
        return pltpu.make_async_copy(
            buf_bs.at[p, me_z, part_of[part]], out.at[part_of[part], :, b_rows(p), :], local_b.at[p, part])

    barrier = pltpu.get_barrier_semaphore()
    for axis, me, n in (("py", me_y, PY), ("snap", me_s, S), ("pz", me_z, PZ)):
        for d in range(1, n):
            pl.semaphore_signal(barrier, inc=1, device_id={axis: other(me, d, n)}, device_id_type=MESH)
    pl.semaphore_wait(barrier, PY + S + PZ - 3)

    def a_start(p):
        for f in (0, 2, 1):
            for d in far_first(PY):
                a_copy(p, f, d).start()
            a_local(p, f).start()

    lag = min(3, ZB)
    for p in range(lag):
        a_start(p)
    planes_in = pltpu.make_async_copy(vel.at[0, 1:3], vw, local_v.at[0])
    planes_in.start()
    pairs = ((gx_in, gx), (my_in, my), (gy_in, gy), (sk_in, sk), (tx_in, tx), (ty_in, ty), (gather_in, gather),
             (mx_in.at[:, mult(me_y, XB)], mx))
    tables = [pltpu.make_async_copy(src, dst, local_t.at[t]) for t, (src, dst) in enumerate(pairs)]
    for table in tables:
        table.start()
    for part in (yh, yl):
        part[:, RY + 2 * NUMS :, :] = jnp.zeros((2, 16 - 2 * NUMS, K * XB), BF16)

    planes_in.wait()
    tables[0].wait()
    lane = lax.broadcasted_iota(jnp.int32, (YB, LANES), 1)
    for f in range(2):
        for p in range(ZB):
            j = 2 * p + f
            line = vw[f, p].reshape(YB, z["NX"])
            ef[j] = dot(line, gx[0]) + dot(line, gx[1])
    for b in range(PY):
        total = jnp.zeros((YB, LANES), F32)
        for j in range(2 * ZB):
            shifted = pltpu.roll(ef[j], (NUMS * (j - b)) % LANES, 1)
            total = jnp.where((lane >= NUMS * j) & (lane < NUMS * (j + 1)), shifted, total)
        half = RY // 2
        for h in range(H):
            upper, lower = total[RY * h : RY * h + half], total[RY * h + half : RY * (h + 1)]
            both = jnp.where(lane[:half] < LANES // 2, upper, pltpu.roll(lower, LANES // 2, 1))
            es[b, half * h : half * (h + 1), :] = both.astype(BF16)
    for d in far_first(PY):
        e_copy(d).start()
    e_local().start()

    for p in range(lag, ZB):
        a_start(p)
    tables[1].wait()
    for r in range(RY):
        scale_y[r : r + 1, :] = jnp.full((1, XB), my[me_s * RY + r], F32)
    tables[2].wait()

    def arrived(p, f):
        a_local(p, f).wait()
        for d in far_first(PY):
            a_copy(p, f, d).wait_recv()

    def go_on(p, f):
        for d in far_first(S):
            c_copy(p, f, d).start()
        c_local(p, f).start()

    def a_stage(p):
        arrived(p, 0)
        go_on(p, 0)
        arrived(p, 2)
        vel_u, vel_w = (buf_a[p, f].reshape(z["NY"], XB) for f in range(2))
        numbers = (dot(gy[0, 0], vel_u) + dot(gy[1, 0], vel_u)) + (dot(gy[0, 1], vel_w) + dot(gy[1, 1], vel_w))
        for s in range(S):
            buf_v[p, s, RY:, :] = numbers[2 * NUMS * s : 2 * NUMS * (s + 1)].astype(BF16)
        arrived(p, 1)
        go_on(p, 1)

    def e_stage():
        e_local().wait()
        for d in far_first(PY):
            e_copy(d).wait_recv()
        for d in far_first(S):
            ce_copy(d).start()
        ce_local().start()

    def se_stage():
        for table in tables[3:]:
            table.wait()
        ce_local().wait()
        for d in far_first(S):
            ce_copy(d).wait_recv()
        for k in range(K):
            total = sk[k, 0] * buf_ce[0].astype(F32)
            for s in range(1, S):
                total = total + sk[k, s] * buf_ce[s].astype(F32)
            se[RY * k : RY * k + RY // 2, :] = total
            se[RY * k + RY // 2 : RY * (k + 1), :] = pltpu.roll(total, LANES // 2, 1)

    def sketch(parts, k):
        total = sk[k, 0] * parts[0]
        for s in range(1, S):
            total = total + sk[k, s] * parts[s]
        return halves(total)

    def sketch_field(p, f):
        for t in range(RY // 16):
            rows = slice(16 * t, 16 * (t + 1))
            parts = [(buf_cv[s, p, rows, :] if f == 1 else buf_c[s, p, f // 2, rows, :]).astype(F32) for s in range(S)]
            for k in range(K):
                high, low = sketch(parts, k)
                own = slice(RY * k + 16 * t, RY * k + 16 * (t + 1))
                if f != 1:
                    yh[f // 2, rows, XB * k : XB * (k + 1)] = high
                    yl[f // 2, rows, XB * k : XB * (k + 1)] = low
                if f != 0:
                    xh[f - 1, own, :XB] = high
                    xl[f - 1, own, :XB] = low
                if f != 2:
                    pb[2 * f, own, :] = high
                    pb[2 * f + 1, own, :] = low

    def x_slope(f):
        return dot(xh[f], tx[0, f]) + dot(xl[f], tx[0, f]) + dot(xh[f], tx[1, f])

    def y_slope(f):
        return dot(ty[0, f], yh[f]) + dot(ty[0, f], yl[f]) + dot(ty[1, f], yh[f])

    def send_part(p, part):
        for f in range(part_of[part].start, part_of[part].stop):
            moved = dot(gather[...], pb[f]).astype(BF16)
            for q in range(PZ):
                for g in range(groups):
                    cut = (q * groups + g) * 8
                    buf_bs[p, q, f, g] = moved[cut : cut + 8]
        for d in far_first(PZ):
            b_copy(p, part, d).start()
        b_local(p, part).start()

    def sketch_numbers(p, f):
        parts = [buf_cv[s, p, RY:, :].astype(F32) for s in range(S)]
        for k in range(K):
            high, low = sketch(parts, k)
            yh[f, RY : RY + 2 * NUMS, XB * k : XB * (k + 1)] = high
            yl[f, RY : RY + 2 * NUMS, XB * k : XB * (k + 1)] = low
        high, low = halves(pltpu.roll(se[...], lax.rem(LANES - 2 * NUMS * p, LANES), 1))
        xh[f, :, XB:] = high
        xl[f, :, XB:] = low

    def came(p, f):
        c_local(p, f).wait()
        for d in far_first(S):
            c_copy(p, f, d).wait_recv()

    def uv_stage(p):
        came(p, 0)
        sketch_field(p, 0)
        came(p, 1)
        sketch_field(p, 1)
        sketch_numbers(p, 0)
        x_slopes, y_slopes = x_slope(0), y_slope(0)
        for k in range(K):
            own, cols = slice(RY * k, RY * (k + 1)), slice(XB * k, XB * (k + 1))
            pb[4, own, :] = (x_slopes[own] * mx[...] - y_slopes[:, cols] * scale_y[...]).astype(BF16)
        send_part(p, 0)

    def w_stage(p):
        came(p, 2)
        sketch_field(p, 2)
        sketch_numbers(p, 1)
        x_slopes, y_slopes = x_slope(1), y_slope(1)
        for k in range(K):
            own, cols = slice(RY * k, RY * (k + 1)), slice(XB * k, XB * (k + 1))
            pb[5, own, :] = (x_slopes[own] * mx[...]).astype(BF16)
            pb[6, own, :] = (y_slopes[:, cols] * scale_y[...]).astype(BF16)
        send_part(p, 1)

    @pl.loop(0, ZB + lag + 1)
    def _(i):
        @pl.when(i < ZB)
        def _():
            a_stage(i)

        @pl.when((i >= 1) & (i <= ZB))
        def _():
            go_on(i - 1, 2)

        @pl.when(i == lag - 1)
        def _():
            e_stage()

        @pl.when(i == lag)
        def _():
            se_stage()

        @pl.when((i >= lag) & (i < ZB + lag))
        def _():
            uv_stage(i - lag)

        @pl.when(i > lag)
        def _():
            w_stage(i - lag - 1)

    for p in range(ZB):
        for part in range(2):
            b_local(p, part).wait()
            for d in far_first(PZ):
                b_copy(p, part, d).wait_recv()

    for p in range(ZB):
        for f in range(3):
            for d in far_first(PY):
                a_copy(p, f, d).wait_send()
            for d in far_first(S):
                c_copy(p, f, d).wait_send()
        for part in range(2):
            for d in far_first(PZ):
                b_copy(p, part, d).wait_send()
    for d in far_first(PY):
        e_copy(d).wait_send()
    for d in far_first(S):
        ce_copy(d).wait_send()


def z_body(z, lines, dz, turn, mz, out):
    K, NZ, XB = z["K"], z["NZ"], z["XB"]
    same = lax.broadcasted_iota(jnp.int32, (NZ, NZ), 0) == lax.broadcasted_iota(jnp.int32, (NZ, NZ), 1)
    scale_z = jnp.broadcast_to(jnp.sum(jnp.where(same, mz[...], 0.0), axis=1, keepdims=True), (NZ, XB))
    slope = [dot(dz[0], lines[2 * f]) + dot(dz[0], lines[2 * f + 1]) + dot(dz[1], lines[2 * f]) for f in range(2)]
    w_x, w_y, spin_z = (dot(turn[...], lines[f]) for f in (5, 6, 4))
    for i in range(8):
        r, k = divmod(i, K)
        cut = slice(NZ * i, NZ * (i + 1))
        out[k, 0, r] = w_y[cut] - slope[1][cut] * scale_z
        out[k, 1, r] = slope[0][cut] * scale_z - w_x[cut]
        out[k, 2, r] = spin_z[cut]


def solution(mesh):
    def step(velocity, metric_x, metric_y, metric_z, sketch_matrix):
        whole = (1, 3, velocity.shape[2] * mesh.shape["pz"], velocity.shape[3] * mesh.shape["py"], velocity.shape[4])
        z = sizes_of(mesh, whole, sketch_matrix.shape[1])
        S, PY, PZ, K, ZB, YB, XB, RY, RG, NX, NY, NZ = (z[n] for n in (
            "S", "PY", "PZ", "K", "ZB", "YB", "XB", "RY", "RG", "NX", "NY", "NZ"))
        tables, z_tables = tables_of(z)
        groups, fields = K * RG // 8, 7
        dma = pltpu.SemaphoreType.DMA
        anywhere = pl.BlockSpec(memory_space=pl.ANY)
        lines = pl.pallas_call(
            functools.partial(body, z),
            out_shape=jax.ShapeDtypeStruct((fields, groups, 8 * NZ, XB), BF16),
            in_specs=[anywhere] * 9,
            out_specs=anywhere,
            scratch_shapes=[pltpu.VMEM(t.shape, t.dtype) for t in tables] + [
                pltpu.VMEM((1, XB), F32),
                pltpu.SMEM((NY,), F32),
                pltpu.SMEM((K, S), F32),
                pltpu.VMEM((RY, XB), F32),
                pltpu.VMEM((2, ZB, YB // RY, RY, NX), BF16),
                pltpu.VMEM((2 * ZB, YB, LANES), F32),
                pltpu.VMEM((PY, YB // 2, LANES), BF16),
                pltpu.VMEM((ZB, 2, S, RY, XB), BF16),
                pltpu.VMEM((ZB, S, RY + 2 * NUMS, XB), BF16),
                pltpu.VMEM((NY // 2, LANES), BF16),
                pltpu.VMEM((S, ZB, 2, RY, XB), BF16),
                pltpu.VMEM((S, ZB, RY + 2 * NUMS, XB), BF16),
                pltpu.VMEM((S, RY // 2, LANES), BF16),
                pltpu.VMEM((K * RY, LANES), F32),
                pltpu.VMEM((2, K * RY, XB + LANES), BF16),
                pltpu.VMEM((2, K * RY, XB + LANES), BF16),
                pltpu.VMEM((2, RY + 16, K * XB), BF16),
                pltpu.VMEM((2, RY + 16, K * XB), BF16),
                pltpu.VMEM((fields, K * RY, XB), BF16),
                pltpu.VMEM((ZB, PZ, fields, groups, 8, XB), BF16),
                dma((ZB, 3, PY - 1)), dma((ZB, 3, PY - 1)), dma((PY - 1,)), dma((PY - 1,)),
                dma((ZB, 3, S - 1)), dma((ZB, 3, S - 1)),
                dma((S - 1,)), dma((S - 1,)), dma((ZB, 2, PZ - 1)), dma((ZB, 2, PZ - 1)),
                dma((8,)), dma((1,)), dma((ZB, 3)), dma((1,)), dma((ZB, 3)), dma((1,)), dma((ZB, 2)),
            ],
            compiler_params=pltpu.CompilerParams(
                collective_id=0, has_side_effects=True, vmem_limit_bytes=56 * 1024 * 1024),
        )(velocity.reshape(1, 3, ZB, YB // RY, RY, NX), *tables, metric_x[None, :], metric_y, sketch_matrix.T)
        per = 8 // K
        whole_block = lambda t: pl.BlockSpec(t.shape, lambda g: (0,) * t.ndim)
        metric_row = metric_z[None, :]
        result = pl.pallas_call(
            functools.partial(z_body, z),
            grid=(groups,),
            out_shape=jax.ShapeDtypeStruct((K, 3, RG, NZ, XB), F32),
            in_specs=[pl.BlockSpec((fields, pl.Squeezed(), 8 * NZ, XB), lambda g: (0, g, 0, 0))] + [whole_block(t) for t in (*z_tables, metric_row)],
            out_specs=pl.BlockSpec((K, 3, per, NZ, XB), lambda g: (0, 0, g, 0, 0)),
        )(lines, *z_tables, metric_row)
        return jnp.swapaxes(result, 2, 3)

    return jax.shard_map(
        step,
        mesh=mesh,
        in_specs=(P("snap", None, "pz", "py", None), P(), P(), P(), P()),
        out_specs=P(None, None, None, ("snap", "pz"), "py"),
        check_vma=False,
    )
```

```python
import functools

import jax
import jax.numpy as jnp
import numpy as np
from jax import lax
from jax.experimental import pallas as pl
from jax.experimental.pallas import tpu as pltpu
from jax.sharding import PartitionSpec as P

MESH = pl.DeviceIdType.MESH
F32 = jnp.float32
BF16 = jnp.bfloat16
LANES = 128
NUMS = 4


def tridiagonal(n):
    return np.eye(n) + (np.eye(n, k=1) + np.eye(n, k=-1)) / 3.0


def right_side(n):
    first = np.eye(n, k=1) - np.eye(n, k=-1)
    second = np.eye(n, k=2) - np.eye(n, k=-2)
    return 7.0 / 9.0 * first + 1.0 / 36.0 * second


def derivative(n):
    return np.linalg.solve(tridiagonal(n), right_side(n))


def block_table(n):
    halo = np.zeros((n, NUMS))
    edge = 7.0 / 9.0 + 1.0 / 36.0
    halo[0, 0], halo[1, 0], halo[0, 1] = -edge, -1.0 / 36.0, 1.0
    halo[n - 1, 2], halo[n - 2, 2], halo[n - 1, 3] = edge, 1.0 / 36.0, 1.0
    return np.linalg.solve(tridiagonal(n), np.concatenate([right_side(n), halo], axis=1))


def interface_rows(n, blocks):
    whole, size = derivative(n), n // blocks
    rows = np.zeros((blocks, NUMS, n))
    for block in range(blocks):
        low, high = block * size, (block + 1) * size
        if block > 0:
            rows[block, 0, low - 1] = 1.0
            rows[block, 1] = -whole[low - 1] / 3.0
            rows[block, 1, low - 1] += 1.0 / 36.0
            rows[block, 1, low - 2] -= 1.0 / 36.0
        if block < blocks - 1:
            rows[block, 2, high] = 1.0
            rows[block, 3] = -whole[high] / 3.0
            rows[block, 3, high + 1] += 1.0 / 36.0
            rows[block, 3, high] -= 1.0 / 36.0
    return rows.reshape(blocks * NUMS, n)


def split(table):
    high = np.asarray(table, np.float32).astype(BF16)
    low = (np.asarray(table, np.float64) - high.astype(np.float64)).astype(BF16)
    return np.stack([high, low])


def dot(left, right):
    return jnp.dot(left, right, preferred_element_type=F32)


def halves(value):
    high = value.astype(BF16)
    return high, (value - high.astype(F32)).astype(BF16)


def far_first(n):
    return sorted(range(1, n), key=lambda d: -min(d, n - d))


def sizes_of(mesh, shape, rank):
    snaps, nyblocks, nzblocks = mesh.shape["snap"], mesh.shape["py"], mesh.shape["pz"]
    nz, ny, nx = shape[2:]
    return dict(
        S=snaps, PY=nyblocks, PZ=nzblocks, K=rank, ZB=nz // nzblocks, YB=ny // nyblocks,
        XB=nx // nyblocks, RY=ny // snaps, RG=ny // snaps // nzblocks, NX=nx, NY=ny, NZ=nz,
    )


def tables_of(z):
    S, PY, PZ, K, RY, RG, XB, NZ = (z[n] for n in ("S", "PY", "PZ", "K", "RY", "RG", "XB", "NZ"))
    gx = np.zeros((z["NX"], LANES))
    gx[:, : PY * NUMS] = interface_rows(z["NX"], PY).T
    numbers_y = interface_rows(z["NY"], S).reshape(S, NUMS, z["NY"])
    gy = np.zeros((2, S, 2, NUMS, z["NY"]))
    gy[0, :, 0] = gy[1, :, 1] = numbers_y
    gy = gy.reshape(2, 2 * NUMS * S, z["NY"])
    bx, by = block_table(XB), block_table(RY)
    tx = np.zeros((2, XB + LANES, XB))
    ty = np.zeros((2, RY, RY + 16))
    for f in range(2):
        tx[f, :XB] = bx[:, :XB].T
        tx[f, XB + NUMS * f : XB + NUMS * (f + 1)] = bx[:, XB:].T
        ty[f, :, :RY] = by[:, :RY]
        ty[f, :, RY + NUMS * f : RY + NUMS * (f + 1)] = by[:, RY:]
    dz = np.einsum("zw,ij->izwj", derivative(NZ), np.eye(8)).reshape(8 * NZ, 8 * NZ)
    turn = np.einsum("zw,ij->izwj", np.eye(NZ), np.eye(8)).reshape(8 * NZ, 8 * NZ)
    gather = np.zeros((K * RY, K * RY))
    groups = K * RG // 8
    for k in range(K):
        for q in range(PZ):
            for r in range(RG):
                g, i = divmod(r * K + k, 8)
                gather[(q * groups + g) * 8 + i, k * RY + q * RG + r] = 1.0
    one = lambda t: jnp.asarray(t.astype(np.float32)).astype(BF16)
    return [jnp.asarray(split(t)) for t in (gx, gy, tx, ty)] + [one(gather)], [jnp.asarray(split(dz)), one(turn)]


def body(
    z, vel, gx_in, gy_in, tx_in, ty_in, gather_in, mx_in, my_in, sk_in, out,
    gx, gy, tx, ty, gather, mx, my, sk, scale_y,
    vw, ef, es, buf_a, buf_v, buf_e, buf_c, buf_cv, buf_ce, se, xh, xl, yh, yl, pb, buf_bs,
    send_a, recv_a, send_e, recv_e, send_c, recv_c, send_ce, recv_ce, send_b, recv_b,
    local_t, local_v, local_a, local_e, local_c, local_ce, local_b,
):
    S, PY, PZ, K, ZB, YB, XB, RY, RG = (z[n] for n in ("S", "PY", "PZ", "K", "ZB", "YB", "XB", "RY", "RG"))
    groups, H = K * RG // 8, YB // RY
    me_s, me_y, me_z = lax.axis_index("snap"), lax.axis_index("py"), lax.axis_index("pz")

    def other(me, d, n):
        return lax.rem(me + d, n)

    def remote(src, dst, send, recv, axis, peer):
        return pltpu.make_async_remote_copy(
            src_ref=src, dst_ref=dst, send_sem=send, recv_sem=recv, device_id={axis: peer}, device_id_type=MESH)

    def mult(value, size):
        return pl.ds(pl.multiple_of(value * size, size), size)

    def a_ends(p, f, peer):
        own = pl.ds(me_y * H, H)
        dst = buf_v.at[p, own, :RY, :] if f == 1 else buf_a.at[p, f // 2, own]
        return vel.at[0, f, p, :, :, mult(peer, XB)], dst

    def a_copy(p, f, d):
        peer = other(me_y, d, PY)
        return remote(*a_ends(p, f, peer), send_a.at[p, f, d - 1], recv_a.at[p, f, d - 1], "py", peer)

    def a_local(p, f):
        return pltpu.make_async_copy(*a_ends(p, f, me_y), local_a.at[p, f])

    def e_copy(d):
        peer = other(me_y, d, PY)
        return remote(es.at[peer], buf_e.at[mult(me_y, YB // 2), :], send_e.at[d - 1], recv_e.at[d - 1], "py", peer)

    def e_local():
        return pltpu.make_async_copy(es.at[me_y], buf_e.at[mult(me_y, YB // 2), :], local_e.at[0])

    def c_ends(p, f, peer):
        if f == 1:
            return buf_v.at[p, peer], buf_cv.at[me_s, p]
        return buf_a.at[p, f // 2, peer], buf_c.at[me_s, p, f // 2]

    def c_copy(p, f, d):
        peer = other(me_s, d, S)
        return remote(*c_ends(p, f, peer), send_c.at[p, f, d - 1], recv_c.at[p, f, d - 1], "snap", peer)

    def c_local(p, f):
        return pltpu.make_async_copy(*c_ends(p, f, me_s), local_c.at[p, f])

    def ce_copy(d):
        peer = other(me_s, d, S)
        return remote(buf_e.at[mult(peer, RY // 2), :], buf_ce.at[me_s], send_ce.at[d - 1], recv_ce.at[d - 1], "snap", peer)

    def ce_local():
        return pltpu.make_async_copy(buf_e.at[mult(me_s, RY // 2), :], buf_ce.at[me_s], local_ce.at[0])

    def b_rows(p):
        return pl.ds(pl.multiple_of((me_z * ZB + p) * 8, 8), 8)

    part_of = (slice(0, 5), slice(5, 6), slice(6, 7))

    def b_copy(p, part, d):
        peer = other(me_z, d, PZ)
        return remote(buf_bs.at[p, peer, part_of[part]], out.at[part_of[part], :, b_rows(p), :],
                      send_b.at[p, part, d - 1], recv_b.at[p, part, d - 1], "pz", peer)

    def b_local(p, part):
        return pltpu.make_async_copy(
            buf_bs.at[p, me_z, part_of[part]], out.at[part_of[part], :, b_rows(p), :], local_b.at[p, part])

    barrier = pltpu.get_barrier_semaphore()
    for axis, me, n in (("py", me_y, PY), ("snap", me_s, S), ("pz", me_z, PZ)):
        for d in range(1, n):
            pl.semaphore_signal(barrier, inc=1, device_id={axis: other(me, d, n)}, device_id_type=MESH)
    pl.semaphore_wait(barrier, PY + S + PZ - 3)

    def a_start(p):
        for f in (0, 2, 1):
            for d in far_first(PY):
                a_copy(p, f, d).start()
            a_local(p, f).start()

    lag = min(3, ZB)
    for p in range(lag):
        a_start(p)
    planes_in = pltpu.make_async_copy(vel.at[0, 1:3], vw, local_v.at[0])
    planes_in.start()
    pairs = ((gx_in, gx), (my_in, my), (gy_in, gy), (sk_in, sk), (tx_in, tx), (ty_in, ty), (gather_in, gather),
             (mx_in.at[:, mult(me_y, XB)], mx))
    tables = [pltpu.make_async_copy(src, dst, local_t.at[t]) for t, (src, dst) in enumerate(pairs)]
    for table in tables:
        table.start()
    for part in (yh, yl):
        part[:, RY + 2 * NUMS :, :] = jnp.zeros((2, 16 - 2 * NUMS, K * XB), BF16)

    planes_in.wait()
    tables[0].wait()
    lane = lax.broadcasted_iota(jnp.int32, (YB, LANES), 1)
    for f in range(2):
        for p in range(ZB):
            j = 2 * p + f
            line = vw[f, p].reshape(YB, z["NX"])
            ef[j] = dot(line, gx[0]) + dot(line, gx[1])
    for b in range(PY):
        total = jnp.zeros((YB, LANES), F32)
        for j in range(2 * ZB):
            shifted = pltpu.roll(ef[j], (NUMS * (j - b)) % LANES, 1)
            total = jnp.where((lane >= NUMS * j) & (lane < NUMS * (j + 1)), shifted, total)
        half = RY // 2
        for h in range(H):
            upper, lower = total[RY * h : RY * h + half], total[RY * h + half : RY * (h + 1)]
            both = jnp.where(lane[:half] < LANES // 2, upper, pltpu.roll(lower, LANES // 2, 1))
            es[b, half * h : half * (h + 1), :] = both.astype(BF16)
    for d in far_first(PY):
        e_copy(d).start()
    e_local().start()

    for p in range(lag, ZB):
        a_start(p)
    tables[1].wait()
    for r in range(RY):
        scale_y[r : r + 1, :] = jnp.full((1, XB), my[me_s * RY + r], F32)
    tables[2].wait()

    def arrived(p, f):
        a_local(p, f).wait()
        for d in far_first(PY):
            a_copy(p, f, d).wait_recv()

    def go_on(p, f):
        for d in far_first(S):
            c_copy(p, f, d).start()
        c_local(p, f).start()

    def a_stage(p):
        arrived(p, 0)
        go_on(p, 0)
        arrived(p, 2)
        vel_u, vel_w = (buf_a[p, f].reshape(z["NY"], XB) for f in range(2))
        numbers = (dot(gy[0, 0], vel_u) + dot(gy[1, 0], vel_u)) + (dot(gy[0, 1], vel_w) + dot(gy[1, 1], vel_w))
        for s in range(S):
            buf_v[p, s, RY:, :] = numbers[2 * NUMS * s : 2 * NUMS * (s + 1)].astype(BF16)
        arrived(p, 1)
        go_on(p, 1)

    def e_stage():
        e_local().wait()
        for d in far_first(PY):
            e_copy(d).wait_recv()
        for d in far_first(S):
            ce_copy(d).start()
        ce_local().start()

    def se_stage():
        for table in tables[3:]:
            table.wait()
        ce_local().wait()
        for d in far_first(S):
            ce_copy(d).wait_recv()
        for k in range(K):
            total = sk[k, 0] * buf_ce[0].astype(F32)
            for s in range(1, S):
                total = total + sk[k, s] * buf_ce[s].astype(F32)
            se[RY * k : RY * k + RY // 2, :] = total
            se[RY * k + RY // 2 : RY * (k + 1), :] = pltpu.roll(total, LANES // 2, 1)

    def sketch(parts, k):
        total = sk[k, 0] * parts[0]
        for s in range(1, S):
            total = total + sk[k, s] * parts[s]
        return halves(total)

    def sketch_field(p, f):
        for t in range(RY // 16):
            rows = slice(16 * t, 16 * (t + 1))
            parts = [(buf_cv[s, p, rows, :] if f == 1 else buf_c[s, p, f // 2, rows, :]).astype(F32) for s in range(S)]
            for k in range(K):
                high, low = sketch(parts, k)
                own = slice(RY * k + 16 * t, RY * k + 16 * (t + 1))
                if f != 1:
                    yh[f // 2, rows, XB * k : XB * (k + 1)] = high
                    yl[f // 2, rows, XB * k : XB * (k + 1)] = low
                if f != 0:
                    xh[f - 1, own, :XB] = high
                    xl[f - 1, own, :XB] = low
                if f != 2:
                    pb[2 * f, own, :] = high
                    pb[2 * f + 1, own, :] = low

    def x_slope(f):
        return dot(xh[f], tx[0, f]) + dot(xl[f], tx[0, f]) + dot(xh[f], tx[1, f])

    def y_slope(f):
        return dot(ty[0, f], yh[f]) + dot(ty[0, f], yl[f]) + dot(ty[1, f], yh[f])

    def send_part(p, part):
        for f in range(part_of[part].start, part_of[part].stop):
            moved = dot(gather[...], pb[f]).astype(BF16)
            for q in range(PZ):
                for g in range(groups):
                    cut = (q * groups + g) * 8
                    buf_bs[p, q, f, g] = moved[cut : cut + 8]
        for d in far_first(PZ):
            b_copy(p, part, d).start()
        b_local(p, part).start()

    def sketch_numbers(p, f):
        parts = [buf_cv[s, p, RY:, :].astype(F32) for s in range(S)]
        for k in range(K):
            high, low = sketch(parts, k)
            yh[f, RY : RY + 2 * NUMS, XB * k : XB * (k + 1)] = high
            yl[f, RY : RY + 2 * NUMS, XB * k : XB * (k + 1)] = low
        high, low = halves(pltpu.roll(se[...], lax.rem(LANES - 2 * NUMS * p, LANES), 1))
        xh[f, :, XB:] = high
        xl[f, :, XB:] = low

    def came(p, f):
        c_local(p, f).wait()
        for d in far_first(S):
            c_copy(p, f, d).wait_recv()

    def uv_stage(p):
        came(p, 0)
        sketch_field(p, 0)
        came(p, 1)
        sketch_field(p, 1)
        sketch_numbers(p, 0)
        x_slopes, y_slopes = x_slope(0), y_slope(0)
        for k in range(K):
            own, cols = slice(RY * k, RY * (k + 1)), slice(XB * k, XB * (k + 1))
            pb[4, own, :] = (x_slopes[own] * mx[...] - y_slopes[:, cols] * scale_y[...]).astype(BF16)
        send_part(p, 0)

    def w_stage(p):
        came(p, 2)
        sketch_field(p, 2)
        sketch_numbers(p, 1)
        x_slopes = x_slope(1)
        for k in range(K):
            own = slice(RY * k, RY * (k + 1))
            pb[5, own, :] = (x_slopes[own] * mx[...]).astype(BF16)
        send_part(p, 1)
        y_slopes = y_slope(1)
        for k in range(K):
            own, cols = slice(RY * k, RY * (k + 1)), slice(XB * k, XB * (k + 1))
            pb[6, own, :] = (y_slopes[:, cols] * scale_y[...]).astype(BF16)
        send_part(p, 2)

    @pl.loop(0, ZB + lag + 1)
    def _(i):
        @pl.when(i < ZB)
        def _():
            a_stage(i)

        @pl.when((i >= 1) & (i <= ZB))
        def _():
            go_on(i - 1, 2)

        @pl.when(i == lag - 1)
        def _():
            e_stage()

        @pl.when(i == lag)
        def _():
            se_stage()

        @pl.when((i >= lag) & (i < ZB + lag))
        def _():
            uv_stage(i - lag)

        @pl.when(i > lag)
        def _():
            w_stage(i - lag - 1)

    for p in range(ZB):
        for part in range(3):
            b_local(p, part).wait()
            for d in far_first(PZ):
                b_copy(p, part, d).wait_recv()

    for p in range(ZB):
        for f in range(3):
            for d in far_first(PY):
                a_copy(p, f, d).wait_send()
            for d in far_first(S):
                c_copy(p, f, d).wait_send()
        for part in range(3):
            for d in far_first(PZ):
                b_copy(p, part, d).wait_send()
    for d in far_first(PY):
        e_copy(d).wait_send()
    for d in far_first(S):
        ce_copy(d).wait_send()


def z_body(z, lines, dz, turn, mz, out):
    K, NZ, XB = z["K"], z["NZ"], z["XB"]
    same = lax.broadcasted_iota(jnp.int32, (NZ, NZ), 0) == lax.broadcasted_iota(jnp.int32, (NZ, NZ), 1)
    scale_z = jnp.broadcast_to(jnp.sum(jnp.where(same, mz[...], 0.0), axis=1, keepdims=True), (NZ, XB))
    slope = [dot(dz[0], lines[2 * f]) + dot(dz[0], lines[2 * f + 1]) + dot(dz[1], lines[2 * f]) for f in range(2)]
    w_x, w_y, spin_z = (dot(turn[...], lines[f]) for f in (5, 6, 4))
    for i in range(8):
        r, k = divmod(i, K)
        cut = slice(NZ * i, NZ * (i + 1))
        out[k, 0, r] = w_y[cut] - slope[1][cut] * scale_z
        out[k, 1, r] = slope[0][cut] * scale_z - w_x[cut]
        out[k, 2, r] = spin_z[cut]


def solution(mesh):
    def step(velocity, metric_x, metric_y, metric_z, sketch_matrix):
        whole = (1, 3, velocity.shape[2] * mesh.shape["pz"], velocity.shape[3] * mesh.shape["py"], velocity.shape[4])
        z = sizes_of(mesh, whole, sketch_matrix.shape[1])
        S, PY, PZ, K, ZB, YB, XB, RY, RG, NX, NY, NZ = (z[n] for n in (
            "S", "PY", "PZ", "K", "ZB", "YB", "XB", "RY", "RG", "NX", "NY", "NZ"))
        tables, z_tables = tables_of(z)
        groups, fields = K * RG // 8, 7
        dma = pltpu.SemaphoreType.DMA
        anywhere = pl.BlockSpec(memory_space=pl.ANY)
        lines = pl.pallas_call(
            functools.partial(body, z),
            out_shape=jax.ShapeDtypeStruct((fields, groups, 8 * NZ, XB), BF16),
            in_specs=[anywhere] * 9,
            out_specs=anywhere,
            scratch_shapes=[pltpu.VMEM(t.shape, t.dtype) for t in tables] + [
                pltpu.VMEM((1, XB), F32),
                pltpu.SMEM((NY,), F32),
                pltpu.SMEM((K, S), F32),
                pltpu.VMEM((RY, XB), F32),
                pltpu.VMEM((2, ZB, YB // RY, RY, NX), BF16),
                pltpu.VMEM((2 * ZB, YB, LANES), F32),
                pltpu.VMEM((PY, YB // 2, LANES), BF16),
                pltpu.VMEM((ZB, 2, S, RY, XB), BF16),
                pltpu.VMEM((ZB, S, RY + 2 * NUMS, XB), BF16),
                pltpu.VMEM((NY // 2, LANES), BF16),
                pltpu.VMEM((S, ZB, 2, RY, XB), BF16),
                pltpu.VMEM((S, ZB, RY + 2 * NUMS, XB), BF16),
                pltpu.VMEM((S, RY // 2, LANES), BF16),
                pltpu.VMEM((K * RY, LANES), F32),
                pltpu.VMEM((2, K * RY, XB + LANES), BF16),
                pltpu.VMEM((2, K * RY, XB + LANES), BF16),
                pltpu.VMEM((2, RY + 16, K * XB), BF16),
                pltpu.VMEM((2, RY + 16, K * XB), BF16),
                pltpu.VMEM((fields, K * RY, XB), BF16),
                pltpu.VMEM((ZB, PZ, fields, groups, 8, XB), BF16),
                dma((ZB, 3, PY - 1)), dma((ZB, 3, PY - 1)), dma((PY - 1,)), dma((PY - 1,)),
                dma((ZB, 3, S - 1)), dma((ZB, 3, S - 1)),
                dma((S - 1,)), dma((S - 1,)), dma((ZB, 3, PZ - 1)), dma((ZB, 3, PZ - 1)),
                dma((8,)), dma((1,)), dma((ZB, 3)), dma((1,)), dma((ZB, 3)), dma((1,)), dma((ZB, 3)),
            ],
            compiler_params=pltpu.CompilerParams(
                collective_id=0, has_side_effects=True, vmem_limit_bytes=56 * 1024 * 1024),
        )(velocity.reshape(1, 3, ZB, YB // RY, RY, NX), *tables, metric_x[None, :], metric_y, sketch_matrix.T)
        per = 8 // K
        whole_block = lambda t: pl.BlockSpec(t.shape, lambda g: (0,) * t.ndim)
        metric_row = metric_z[None, :]
        result = pl.pallas_call(
            functools.partial(z_body, z),
            grid=(groups,),
            out_shape=jax.ShapeDtypeStruct((K, 3, RG, NZ, XB), F32),
            in_specs=[pl.BlockSpec((fields, pl.Squeezed(), 8 * NZ, XB), lambda g: (0, g, 0, 0))] + [whole_block(t) for t in (*z_tables, metric_row)],
            out_specs=pl.BlockSpec((K, 3, per, NZ, XB), lambda g: (0, 0, g, 0, 0)),
        )(lines, *z_tables, metric_row)
        return jnp.swapaxes(result, 2, 3)

    return jax.shard_map(
        step,
        mesh=mesh,
        in_specs=(P("snap", None, "pz", "py", None), P(), P(), P(), P()),
        out_specs=P(None, None, None, ("snap", "pz"), "py"),
        check_vma=False,
    )
```
